512 devices in a mesh: ctx: 128 (over y_lo, z, x), head: 4 (over y_hi, core).
Axes of the slice: x: 4, y: 8 (y_hi: 2, y_lo: 4; y = y_hi * 4 + y_lo), z: 8, core: 2. Of those that a mesh axis runs over, the one named last changes fastest.
Arguments:
- queries: bfloat16 [65536, 1024], P('ctx', 'head'), may hold values from -40 to 40
- keys: bfloat16 [65536, 1024], P('ctx', 'head'), may hold values from -40 to 40
- values: bfloat16 [65536, 1024], P('ctx', 'head'), may hold values from -6 to 6
- out_weight: bfloat16 [1024, 1024], P('head'), may hold values from -0.1875 to 0.1875
- grad_output: bfloat16 [65536, 1024], P('ctx', 'head'), may hold values from -6 to 6
- key_lists: int32 [512, 8], replicated, may hold values from 0 to 511, as said below
- key_counts: int32 [512], replicated, may hold values from 1 to 8, as said below
Outputs:
- output: bfloat16 [65536, 1024], P('ctx', 'head')
- grad_queries: bfloat16 [65536, 1024], P('ctx', 'head')
- grad_keys: bfloat16 [65536, 1024], P('ctx', 'head')
- grad_values: bfloat16 [65536, 1024], P('ctx', 'head')
- grad_weight: float32 [1024, 1024], P('head')
The draws below stay inside these ranges and needn't reach their ends.
Inputs may be any that keep to these rules, and one draw needn't show every extreme that they name: `key_lists`: row a names 8 different key blocks, all among the 12 blocks from 4 * (a // 4 - 1) on, counted modulo 512; its first entry is a itself, its second lies among the first 4 of those blocks, its third among the last 4. `key_counts`: every query block whose index is a multiple of 4 uses all 8 slots.
All inputs are finite; a program needn't handle non-finite values.
Results may differ from the reference program's by a relative error of at most 0.029.
Values may be sent and summed in bfloat16 or wider, within the bound.
A program may use at most 128 MiB of HBM per device.

```python
import jax
import jax.numpy as jnp
from jax import lax

HEADS = 8
HD = 128
D = 1024
BLK = 128
NSEL = 8
NB_DEV = 4
NBLK = 512
TOKENS = 65536


def draw_queries(key, part):
    result = 1.5 * jnp.clip(jax.random.normal(jax.random.fold_in(key, 2), (TOKENS, D), jnp.float32), -6.0, 6.0)
    return result.astype(jnp.bfloat16)


def draw_keys(key, part):
    result = 1.5 * jnp.clip(jax.random.normal(jax.random.fold_in(key, 3), (TOKENS, D), jnp.float32), -6.0, 6.0)
    return result.astype(jnp.bfloat16)


def draw_key_lists(key, part):
    window_size = 3 * NB_DEV
    block_ids = jnp.arange(NBLK, dtype=jnp.int32)
    owner = block_ids // NB_DEV
    own_slot = NB_DEV + block_ids % NB_DEV
    lower_slot = jax.random.randint(jax.random.fold_in(key, 11), (NBLK,), 0, NB_DEV).astype(jnp.int32)
    upper_slot = 2 * NB_DEV + jax.random.randint(jax.random.fold_in(key, 13), (NBLK,), 0, NB_DEV).astype(jnp.int32)
    row_keys = jax.random.split(jax.random.fold_in(key, 5), NBLK)
    orders = jax.vmap(lambda row_key: jax.random.permutation(row_key, window_size - 1))(row_keys).astype(jnp.int32)
    others = orders + (orders >= own_slot[:, None]).astype(jnp.int32)
    flagged = ((others == lower_slot[:, None]) | (others == upper_slot[:, None])).astype(jnp.int32)
    ranking = flagged * window_size + jnp.arange(window_size - 1, dtype=jnp.int32)[None, :]
    order_ids = jnp.argsort(ranking, axis=1, stable=True).astype(jnp.int32)
    remaining = jnp.take_along_axis(others, order_ids, axis=1)
    slots = jnp.concatenate([own_slot[:, None], lower_slot[:, None], upper_slot[:, None], remaining[:, :NSEL - 3]], axis=1)
    return ((owner[:, None] - 1) * NB_DEV + slots) % NBLK


def draw_key_counts(key, part):
    counts = jax.random.randint(jax.random.fold_in(key, 7), (NBLK,), 1, NSEL + 1).astype(jnp.int32)
    leading = jnp.arange(NBLK, dtype=jnp.int32) % NB_DEV == 0
    return jnp.where(leading, NSEL, counts).astype(jnp.int32)


def shard_levels(own_key, shape, shards, smallest, top_value):
    factor_of, own = 1.0, jax.random.fold_in(own_key, 6)
    for position, blocks in shards:
        draws = jnp.exp(jax.random.uniform(jax.random.fold_in(own, position), (blocks,), jnp.float32, smallest / len(shards), top_value / len(shards)))
        factor_of = factor_of * jnp.repeat(draws, shape[position] // blocks).reshape([-1 if axis == position else 1 for axis in range(len(shape))])
    return factor_of


def bell_draw(stream_key, shape, deviation, bound, pieces=(), kind=jnp.bfloat16):
    values = jax.random.normal(stream_key, shape, jnp.float32) * deviation
    if len(pieces) > 0:
        values = shard_levels(stream_key, shape, pieces, -0.22, 0.18) * values
    return jnp.clip(values, min=-bound, max=bound).astype(kind)


def setup_inputs(seed: int = 0) -> dict:
    arg_keys = jax.random.split(jax.random.key(seed), 8)
    return {
        "queries": draw_queries(jax.random.fold_in(arg_keys[7], 71), 0),
        "keys": draw_keys(jax.random.fold_in(arg_keys[7], 71), 0),
        "values": bell_draw(arg_keys[2], (TOKENS, D), 1.0, 6.0, ((0, 128), (1, 4))),
        "out_weight": bell_draw(arg_keys[3], (D, D), D ** -0.5, 0.1875, ((0, 4),)),
        "grad_output": bell_draw(arg_keys[4], (TOKENS, D), 1.0, 6.0, ((0, 128), (1, 4))),
        "key_lists": draw_key_lists(jax.random.fold_in(arg_keys[7], 71), 0),
        "key_counts": draw_key_counts(jax.random.fold_in(arg_keys[7], 71), 0),
    }


def reference(queries, keys, values, out_weight, grad_output, key_lists, key_counts):
    factor = HD ** -0.5
    query_blocks = queries.reshape(NBLK, BLK, HEADS, HD)
    key_blocks = keys.reshape(NBLK, BLK, HEADS, HD)
    value_blocks = values.reshape(NBLK, BLK, HEADS, HD)
    slot_ids = jnp.arange(NSEL, dtype=jnp.int32)

    def block_scores(block_id):
        chosen = key_lists[block_id]
        usable = slot_ids < key_counts[block_id]
        key_sel = key_blocks[chosen].astype(jnp.float32)
        value_sel = value_blocks[chosen].astype(jnp.float32)
        query_f = query_blocks[block_id].astype(jnp.float32)
        scores = jnp.einsum("ihd,sjhd->hisj", query_f, key_sel) * factor
        scores = jnp.where(usable[None, None, :, None], scores, -jnp.inf)
        return chosen, key_sel, value_sel, query_f, scores

    def forward_block(block_id):
        chosen, key_sel, value_sel, query_f, scores = block_scores(block_id)
        top = jnp.max(scores, axis=(2, 3), keepdims=True)
        log_total = top + jnp.log(jnp.sum(jnp.exp(scores - top), axis=(2, 3), keepdims=True))
        prob_half = lax.optimization_barrier(jnp.exp(scores - log_total).astype(jnp.bfloat16))
        mixed = jnp.einsum("hisj,sjhd->ihd", prob_half.astype(jnp.float32), value_sel)
        return mixed.astype(jnp.bfloat16).reshape(BLK, HEADS * HD), log_total[:, :, 0, 0]

    attn, log_totals = lax.map(forward_block, jnp.arange(NBLK, dtype=jnp.int32))
    attn = attn.reshape(TOKENS, HEADS * HD)
    output = jnp.dot(attn, out_weight, preferred_element_type=jnp.float32).astype(jnp.bfloat16)
    grad_attn = lax.dot_general(grad_output, out_weight, (((1,), (1,)), ((), ())),
                                preferred_element_type=jnp.float32).astype(jnp.bfloat16)
    grad_weight = lax.dot_general(attn, grad_output, (((0,), (0,)), ((), ())),
                                  preferred_element_type=jnp.float32) * (TOKENS ** -0.5)
    row_dots = jnp.sum((grad_attn.astype(jnp.float32) * attn.astype(jnp.float32)).reshape(NBLK, BLK, HEADS, HD), axis=3)
    grad_blocks = grad_attn.reshape(NBLK, BLK, HEADS, HD)

    def backward_step(sums, block_id):
        key_grad, value_grad = sums
        chosen, key_sel, value_sel, query_f, scores = block_scores(block_id)
        probs = jnp.exp(scores - log_totals[block_id][:, :, None, None])
        prob_half = lax.optimization_barrier(probs.astype(jnp.bfloat16)).astype(jnp.float32)
        grad_f = grad_blocks[block_id].astype(jnp.float32)
        grad_probs = jnp.einsum("ihd,sjhd->hisj", grad_f, value_sel)
        dots_here = jnp.transpose(row_dots[block_id])[:, :, None, None]
        grad_scores = lax.optimization_barrier((probs * (grad_probs - dots_here) * factor).astype(jnp.bfloat16))
        grad_scores = grad_scores.astype(jnp.float32)
        query_grad = jnp.einsum("hisj,sjhd->ihd", grad_scores, key_sel)
        key_grad = key_grad.at[chosen].add(jnp.einsum("hisj,ihd->sjhd", grad_scores, query_f))
        value_grad = value_grad.at[chosen].add(jnp.einsum("hisj,ihd->sjhd", prob_half, grad_f))
        return (key_grad, value_grad), query_grad.astype(jnp.bfloat16).reshape(BLK, HEADS * HD)

    zeros_start = jnp.zeros((NBLK, BLK, HEADS, HD), jnp.float32)
    (key_grad, value_grad), query_grads = lax.scan(backward_step, (zeros_start, zeros_start),
                                                   jnp.arange(NBLK, dtype=jnp.int32))
    grad_queries = query_grads.reshape(TOKENS, HEADS * HD)
    grad_keys = key_grad.reshape(TOKENS, HEADS * HD).astype(jnp.bfloat16)
    grad_values = value_grad.reshape(TOKENS, HEADS * HD).astype(jnp.bfloat16)
    return (output, grad_queries, grad_keys, grad_values, grad_weight)
```

```python
import functools

import jax
import jax.numpy as jnp
from jax import lax
from jax.experimental import pallas as pl
from jax.experimental.pallas import tpu as pltpu
from jax.sharding import PartitionSpec as P

HD = 128
BLK = 128
MESH = pl.DeviceIdType.MESH
NY, NZ, NX = 4, 8, 4


def spots():
    pos = lax.axis_index("ctx")
    x = pos % NX
    z = (pos // NX) % NZ
    y = pos // (NX * NZ)
    return y, z, x


def x_peer(d):
    y, z, x = spots()
    p = (x + d) % NX
    return p, {"ctx": (y * NZ + z) * NX + p, "head": lax.axis_index("head")}


def z_peer(d):
    y, z, x = spots()
    p = (z + d) % NZ
    return p, {"ctx": (y * NZ + p) * NX + x, "head": lax.axis_index("head")}


def y_peer(d):
    y, z, x = spots()
    p = (y + d) % NY
    return p, {"ctx": (p * NZ + z) * NX + x, "head": lax.axis_index("head")}


def remote(src, dst, sems, k, device):
    return pltpu.make_async_remote_copy(
        src_ref=src,
        dst_ref=dst,
        send_sem=sems.at[0, k],
        recv_sem=sems.at[1, k],
        device_id=device,
        device_id_type=MESH,
    )


def sum_kernel(scale, part_ref, out_ref, part, xr, s1, zr, s2, yr, gy, gz, gx, sx, sz, sy, ty, tz, tx):
    y, z, x = spots()
    barrier = pltpu.get_barrier_semaphore()
    peers = [x_peer(d) for d in range(1, NX)] + [z_peer(d) for d in range(1, NZ)]
    peers += [y_peer(d) for d in range(1, NY)]
    for _, device in peers:
        pl.semaphore_signal(barrier, inc=1, device_id=device, device_id_type=MESH)
    part[...] = part_ref[...].astype(jnp.bfloat16)
    pl.semaphore_wait(barrier, len(peers))

    def run(copies):
        for c in copies:
            c.start()
        for c in copies:
            c.wait()

    rows = lambda i, n: pl.ds(pl.multiple_of(i * n, n), n)
    f32 = jnp.float32
    copies = []
    for d in range(1, NX):
        p, device = x_peer(d)
        copies.append(remote(part.at[rows(p, 64)], xr.at[d - 1], sx, d - 1, device))
    run(copies)
    total = part_ref[rows(x, 64)]
    for d in range(NX - 1):
        total = total + xr[d].astype(f32)
    s1[...] = total.astype(jnp.bfloat16)
    copies = []
    for d in range(1, NZ):
        p, device = z_peer(d)
        copies.append(remote(s1.at[:, rows(p, 128)], zr.at[d - 1], sz, d - 1, device))
    run(copies)
    total = s1[:, rows(z, 128)].astype(f32)
    for d in range(NZ - 1):
        total = total + zr[d].astype(f32)
    s2[...] = total.astype(jnp.bfloat16)
    copies = []
    for d in range(1, NY):
        p, device = y_peer(d)
        copies.append(remote(s2.at[rows(p, 16)], yr.at[d - 1], sy, d - 1, device))
    run(copies)
    total = s2[rows(y, 16)].astype(f32)
    for d in range(NY - 1):
        total = total + yr[d].astype(f32)
    gy[rows(y, 16)] = total.astype(jnp.bfloat16)
    run([
        remote(gy.at[rows(y, 16)], gy.at[rows(y, 16)], ty, d - 1, y_peer(d)[1])
        for d in range(1, NY)
    ])
    gz[:, rows(z, 128)] = gy[...]
    run([
        remote(gy, gz.at[:, rows(z, 128)], tz, d - 1, z_peer(d)[1])
        for d in range(1, NZ)
    ])
    gx[rows(x, 64)] = gz[...]
    run([
        remote(gz, gx.at[rows(x, 64)], tx, d - 1, x_peer(d)[1])
        for d in range(1, NX)
    ])
    out_ref[...] = gx[...].astype(f32) * scale


def ctx_sum(part, scale):
    bf = jnp.bfloat16
    dma = lambda n: pltpu.SemaphoreType.DMA((2, n))
    return pl.pallas_call(
        functools.partial(sum_kernel, scale),
        out_shape=jax.ShapeDtypeStruct(part.shape, jnp.float32),
        in_specs=[pl.BlockSpec(memory_space=pltpu.VMEM)],
        out_specs=pl.BlockSpec(memory_space=pltpu.VMEM),
        scratch_shapes=[
            pltpu.VMEM((256, 1024), bf),
            pltpu.VMEM((NX - 1, 64, 1024), bf),
            pltpu.VMEM((64, 1024), bf),
            pltpu.VMEM((NZ - 1, 64, 128), bf),
            pltpu.VMEM((64, 128), bf),
            pltpu.VMEM((NY - 1, 16, 128), bf),
            pltpu.VMEM((64, 128), bf),
            pltpu.VMEM((64, 1024), bf),
            pltpu.VMEM((256, 1024), bf),
            dma(NX - 1), dma(NZ - 1), dma(NY - 1), dma(NY - 1), dma(NZ - 1), dma(NX - 1),
        ],
        compiler_params=pltpu.CompilerParams(collective_id=0, has_side_effects=True),
        name="ctx_sum",
    )(part)


def with_halo(block, sides, width):
    for axis, dim in sides:
        count = lax.axis_size(axis)
        forward = [(i, i + 1) for i in range(count - 1)]
        forward.append((count - 1, 0))
        backward = [(target, source) for source, target in forward]
        low = lax.ppermute(
            lax.slice_in_dim(block, block.shape[dim] - width, None, axis=dim), axis, forward
        )
        high = lax.ppermute(lax.slice_in_dim(block, 0, width, axis=dim), axis, backward)
        block = jnp.concatenate([low, block, high], axis=dim)
    return block


def block_scores(query_sel, key_sel, usable, factor):
    scores = (
        jnp.einsum("nihd,nsjhd->nhisj", query_sel, key_sel, preferred_element_type=jnp.float32)
        * factor
    )
    return jnp.where(usable[:, None, None, :, None], scores, -jnp.inf)


def key_side(query_sel, grad_sel, log_total, row_dots, picks, usable, window, factor):
    span = window.shape[1]
    key_sel = window[0][picks]
    value_sel = window[1][picks]
    scores = block_scores(query_sel, key_sel, usable, factor)
    probs = jnp.exp(scores - log_total)
    prob_half = probs.astype(jnp.bfloat16)
    grad_probs = jnp.einsum(
        "nihd,nsjhd->nhisj", grad_sel, value_sel, preferred_element_type=jnp.float32
    )
    grad_scores = (probs * (grad_probs - row_dots) * factor).astype(jnp.bfloat16)
    key_parts = jnp.einsum(
        "nhisj,nihd->nsjhd", grad_scores, query_sel, preferred_element_type=jnp.float32
    )
    value_parts = jnp.einsum(
        "nhisj,nihd->nsjhd", prob_half, grad_sel, preferred_element_type=jnp.float32
    )
    selector = (picks[:, :, None] == jnp.arange(span, dtype=jnp.int32)[None, None, :]).astype(
        jnp.float32
    )
    key_window = jnp.einsum("nsw,nsjhd->wjhd", selector, key_parts, precision=lax.Precision.HIGHEST)
    value_window = jnp.einsum(
        "nsw,nsjhd->wjhd", selector, value_parts, precision=lax.Precision.HIGHEST
    )
    query_grad = None
    query_grad = jnp.einsum(
        "nhisj,nsjhd->nihd", grad_scores, key_sel, preferred_element_type=jnp.float32
    )
    return (query_grad, key_window, value_window)


def shards(queries, keys, values, out_weight, grad_output, key_lists, key_counts):
    tok_rows, features = queries.shape
    heads_here = features // HD
    blocks = tok_rows // BLK
    cycle_size = lax.axis_size("ctx")
    cycle_pos = lax.axis_index("ctx")
    all_blocks = blocks * cycle_size
    factor = HD ** (-0.5)
    window_start = (cycle_pos - 1) * blocks
    slot_ids = jnp.arange(key_lists.shape[1], dtype=jnp.int32)
    stacked = jnp.stack([keys, values])
    window = with_halo(stacked, (("ctx", 1),), tok_rows)
    window = window.reshape(2, 3 * blocks, BLK, heads_here, HD)
    own_lists = lax.dynamic_slice_in_dim(key_lists, cycle_pos * blocks, blocks, 0)
    own_counts = lax.dynamic_slice_in_dim(key_counts, cycle_pos * blocks, blocks, 0)
    picks = (own_lists - window_start) % all_blocks
    usable = slot_ids[None, :] < own_counts[:, None]
    query_sel = queries.reshape(blocks, BLK, heads_here, HD)
    key_sel = window[0][picks]
    value_sel = window[1][picks]
    scores = block_scores(query_sel, key_sel, usable, factor)
    top_score = jnp.max(scores, axis=(3, 4), keepdims=True)
    log_total = top_score + jnp.log(
        jnp.sum(jnp.exp(scores - top_score), axis=(3, 4), keepdims=True)
    )
    prob_half = jnp.exp(scores - log_total).astype(jnp.bfloat16)
    mixed = jnp.einsum(
        "nhisj,nsjhd->nihd", prob_half, value_sel, preferred_element_type=jnp.float32
    )
    attn = mixed.astype(jnp.bfloat16).reshape(tok_rows, features)
    partial_out = jnp.dot(attn, out_weight, preferred_element_type=jnp.float32)
    output = lax.psum_scatter(
        partial_out.astype(jnp.bfloat16), "head", scatter_dimension=1, tiled=True
    )
    column_block = lax.all_gather(grad_output, "head", axis=1, tiled=True)
    back_sum = lax.dot_general(
        column_block, out_weight, (((1,), (1,)), ((), ())), preferred_element_type=jnp.float32
    )
    product = lax.dot_general(
        attn, column_block, (((0,), (0,)), ((), ())), preferred_element_type=jnp.float32
    )
    weight_part = product
    back_sum, weight_part = (back_sum, weight_part)
    grad_attn = back_sum.astype(jnp.bfloat16)
    grad_weight = ctx_sum(weight_part, (cycle_size * tok_rows) ** (-0.5))
    dots_rows = jnp.sum(
        (grad_attn.astype(jnp.float32) * attn.astype(jnp.float32)).reshape(
            blocks, BLK, heads_here, HD
        ),
        axis=3,
    )
    row_dots = jnp.transpose(dots_rows, (0, 2, 1))
    grad_sel = grad_attn.reshape(blocks, BLK, heads_here, HD)
    query_grad, key_window, value_window = key_side(
        query_sel, grad_sel, log_total, row_dots[..., None, None], picks, usable, window, factor
    )
    parts = jnp.stack([key_window, value_window]).reshape(2, 3 * tok_rows, features)
    outgoing = jnp.concatenate([parts[:, :tok_rows], parts[:, 2 * tok_rows :]], axis=1)
    returned = with_halo(outgoing.astype(jnp.bfloat16), (("ctx", 1),), tok_rows).astype(
        outgoing.dtype
    )
    summed = (
        parts[:, tok_rows : 2 * tok_rows] + returned[:, :tok_rows] + returned[:, 3 * tok_rows :]
    )
    grad_queries = query_grad.astype(jnp.bfloat16).reshape(tok_rows, features)
    return (
        output,
        grad_queries,
        summed[0].astype(jnp.bfloat16),
        summed[1].astype(jnp.bfloat16),
        grad_weight,
    )


def solution(mesh):
    in_specs = (
        P("ctx", "head"),
        P("ctx", "head"),
        P("ctx", "head"),
        P("head", None),
        P("ctx", "head"),
        P(),
        P(),
    )
    out_specs = (
        P("ctx", "head"),
        P("ctx", "head"),
        P("ctx", "head"),
        P("ctx", "head"),
        P("head", None),
    )
    return jax.shard_map(shards, mesh=mesh, in_specs=in_specs, out_specs=out_specs, check_vma=False)
```

```python
import jax
import jax.numpy as jnp
from jax import lax
from jax.experimental import pallas as pl
from jax.experimental.pallas import tpu as pltpu
from jax.sharding import PartitionSpec as P

HD = 128
BLK = 128
MESH = pl.DeviceIdType.MESH
BF = jnp.bfloat16
F32 = jnp.float32
NY, NZ, NX = 4, 8, 4
NCTX = NY * NZ * NX
LOG2E = 1.4426950408889634
HEADS_HERE = 2
ROWS = 512
WINDOW = 3 * ROWS
CHUNK = 256


def dot(a, b, ca, cb):
    return lax.dot_general(a, b, (((ca,), (cb,)), ((), ())), preferred_element_type=F32)


def span(i, n):
    return pl.ds(pl.multiple_of(i * n, n), n)


def layer_kernel(
    q_ref, k_ref, v_ref, w_ref, g_ref, lists_ref, counts_ref,
    out_ref, dq_ref, dk_ref, dv_ref, dw_ref,
    kw, vw, bias, st, pt, dst, attn, ga, gfull,
    rs_send, rs_recv, rs_keep, rs2_send, rs2_recv,
    ret_send, ret_recv, own_grad,
    part32, part, xr, s1, zr, s2, yr, gy, gz, gx,
    halo_sem, head_sem, rs_sem, ret_sem, sx, sz, sy, ty, tz, tx,
):
    pos = lax.axis_index("ctx")
    hi = lax.axis_index("head")
    x = pos % NX
    z = (pos // NX) % NZ
    y = pos // (NX * NZ)
    core = hi % 2
    far = hi // 2

    def at(ctx, head):
        return {"ctx": ctx, "head": head}

    right = at((pos + 1) % NCTX, hi)
    left = at((pos + NCTX - 1) % NCTX, hi)
    mate = far * 2 + (1 - core)
    twin = (1 - far) * 2 + core
    mate_twin = (1 - far) * 2 + (1 - core)
    to_mate, to_twin = at(pos, mate), at(pos, twin)

    def x_peer(d):
        p = (x + d) % NX
        return p, at((y * NZ + z) * NX + p, hi)

    def z_peer(d):
        p = (z + d) % NZ
        return p, at((y * NZ + p) * NX + x, hi)

    def y_peer(d):
        p = (y + d) % NY
        return p, at((p * NZ + z) * NX + x, hi)

    started = []

    def send(src, dst_, sems, k, device):
        c = pltpu.make_async_remote_copy(
            src_ref=src, dst_ref=dst_, send_sem=sems.at[0, k], recv_sem=sems.at[1, k],
            device_id=device, device_id_type=MESH,
        )
        c.start()
        started.append(c)
        return c

    barrier = pltpu.get_barrier_semaphore()
    peers = [right, left, to_mate, to_twin]
    peers += [x_peer(d)[1] for d in range(1, NX)]
    peers += [z_peer(d)[1] for d in range(1, NZ)]
    peers += [y_peer(d)[1] for d in range(1, NY)]
    for device in peers:
        pl.semaphore_signal(barrier, inc=1, device_id=device, device_id_type=MESH)

    slot = lax.broadcasted_iota(jnp.int32, (1, 8), 1)
    for n in range(4):
        row = lists_ref[pl.ds(pos * 4 + n, 1), :]
        used = slot < counts_ref[pos * 4 + n]
        for wb in range(12):
            block = ((pos + NCTX - 1) * 4 + wb) % (NCTX * 4)
            hit = jnp.where(used & (row == block), 1.0, 0.0)
            hit = jnp.max(hit, axis=1, keepdims=True)
            value = jnp.where(hit > 0.5, 0.0, -jnp.inf)
            bias[wb : wb + 1, n * BLK : (n + 1) * BLK] = jnp.broadcast_to(value, (1, BLK))
    kw[ROWS : 2 * ROWS] = k_ref[...]
    vw[ROWS : 2 * ROWS] = v_ref[...]
    gfull[:, span(hi, 256)] = g_ref[...]
    pl.semaphore_wait(barrier, len(peers))

    halo = [
        send(k_ref, kw.at[0:ROWS], halo_sem, 0, right),
        send(k_ref, kw.at[2 * ROWS : 3 * ROWS], halo_sem, 1, left),
    ]
    g_twin = send(g_ref, gfull.at[:, span(hi, 256)], head_sem, 0, to_twin)
    halo += [
        send(v_ref, vw.at[0:ROWS], halo_sem, 2, right),
        send(v_ref, vw.at[2 * ROWS : 3 * ROWS], halo_sem, 3, left),
    ]
    g_mate = send(g_ref, gfull.at[:, span(hi, 256)], head_sem, 1, to_mate)

    factor = HD ** (-0.5)

    def score_chunk(h, c):
        hc = slice(h * HD, (h + 1) * HD)
        s = dot(kw[c * CHUNK : (c + 1) * CHUNK, hc], q_ref[:, hc], 1, 1) * (factor * LOG2E)
        for b in range(CHUNK // BLK):
            wb = c * (CHUNK // BLK) + b
            st[h, wb * BLK : (wb + 1) * BLK] = s[b * BLK : (b + 1) * BLK] + bias[wb : wb + 1]

    for h in range(HEADS_HERE):
        for c in (2, 3):
            score_chunk(h, c)
    halo[0].wait_recv()
    for h in range(HEADS_HERE):
        for c in (0, 1):
            score_chunk(h, c)
    halo[1].wait_recv()
    for h in range(HEADS_HERE):
        for c in (4, 5):
            score_chunk(h, c)
    for h in range(HEADS_HERE):
        top = jnp.max(st[h], axis=0, keepdims=True)
        total = jnp.zeros((1, ROWS), F32)
        for c in range(WINDOW // CHUNK):
            keys = slice(c * CHUNK, (c + 1) * CHUNK)
            e = jnp.exp2(st[h, keys] - top)
            st[h, keys] = e
            total = total + jnp.sum(e, axis=0, keepdims=True)
        inverse = 1.0 / total
        for c in range(WINDOW // CHUNK):
            keys = slice(c * CHUNK, (c + 1) * CHUNK)
            pt[h, keys] = (st[h, keys] * inverse).astype(BF)
    halo[2].wait_recv()
    halo[3].wait_recv()
    attn_t = []
    for h in range(HEADS_HERE):
        hc = slice(h * HD, (h + 1) * HD)
        mixed = dot(vw[:, hc], pt[h], 0, 0)
        attn_t.append(mixed.astype(BF))
        attn[:, hc] = jnp.transpose(mixed).astype(BF)

    g_twin.wait_recv()
    g_relay = send(
        gfull.at[:, span(twin, 256)], gfull.at[:, span(twin, 256)], head_sem, 2, to_mate
    )
    for f in range(2):
        cols = span(f * 2 + (1 - core), 256)
        rs_send[f] = dot(attn[...], w_ref[:, cols], 1, 0).astype(BF)
    rs = [send(rs_send.at[f], rs_recv.at[f], rs_sem, f, to_mate) for f in range(2)]
    for f in range(2):
        cols = span(f * 2 + core, 256)
        rs_keep[f] = dot(attn[...], w_ref[:, cols], 1, 0)
    g_mate.wait_recv()
    g_relay.wait_recv()

    for h in range(HEADS_HERE):
        value = dot(attn_t[h], gfull[...], 1, 0)
        part32[h * HD : (h + 1) * HD] = value
        part[h * HD : (h + 1) * HD] = value.astype(BF)
    xs = []
    for d in range(1, NX):
        p, device = x_peer(d)
        xs.append(send(part.at[span(p, 64)], xr.at[d - 1], sx, d - 1, device))

    row_dots = []
    for h in range(HEADS_HERE):
        hc = slice(h * HD, (h + 1) * HD)
        back = dot(w_ref[hc], gfull[...], 1, 1).astype(BF).astype(F32)
        row_dots.append(jnp.sum(back * attn_t[h].astype(F32), axis=0, keepdims=True))
        ga[:, hc] = jnp.transpose(back).astype(BF)

    for c in rs:
        c.wait_recv()
    rs2_send[...] = (rs_keep[1 - far] + rs_recv[1 - far].astype(F32)).astype(BF)
    rs2 = send(rs2_send, rs2_recv, rs_sem, 2, to_twin)

    def back_chunk(h, c):
        hc = slice(h * HD, (h + 1) * HD)
        keys = slice(c * CHUNK, (c + 1) * CHUNK)
        dp = dot(vw[keys, hc], ga[:, hc], 1, 1)
        ds = pt[h, keys].astype(F32) * ((dp - row_dots[h]) * factor)
        dst[h, keys] = ds.astype(BF)

    def key_grads(h, side):
        hc = slice(h * HD, (h + 1) * HD)
        keys = slice(side * ROWS, (side + 1) * ROWS)
        return dot(dst[h, keys], q_ref[:, hc], 1, 0), dot(pt[h, keys], ga[:, hc], 1, 0)

    rets = []
    for i, side, device in ((0, 2, right), (1, 0, left)):
        for h in range(HEADS_HERE):
            hc = slice(h * HD, (h + 1) * HD)
            for c in (side * 2, side * 2 + 1):
                back_chunk(h, c)
            dk, dv = key_grads(h, side)
            ret_send[i, 0, :, hc] = dk.astype(BF)
            ret_send[i, 1, :, hc] = dv.astype(BF)
        rets.append(send(ret_send.at[i], ret_recv.at[i], ret_sem, i, device))

    for c in xs:
        c.wait_recv()
    total = part32[span(x, 64)]
    for d in range(NX - 1):
        total = total + xr[d].astype(F32)
    s1[...] = total.astype(BF)
    zs = []
    for d in range(1, NZ):
        p, device = z_peer(d)
        zs.append(send(s1.at[:, span(p, 128)], zr.at[d - 1], sz, d - 1, device))

    for h in range(HEADS_HERE):
        hc = slice(h * HD, (h + 1) * HD)
        for c in (2, 3):
            back_chunk(h, c)
        dk, dv = key_grads(h, 1)
        own_grad[0, :, hc] = dk
        own_grad[1, :, hc] = dv

    for c in zs:
        c.wait_recv()
    total = s1[:, span(z, 128)].astype(F32)
    for d in range(NZ - 1):
        total = total + zr[d].astype(F32)
    s2[...] = total.astype(BF)
    ys = []
    for d in range(1, NY):
        p, device = y_peer(d)
        ys.append(send(s2.at[span(p, 16)], yr.at[d - 1], sy, d - 1, device))

    for h in range(HEADS_HERE):
        hc = slice(h * HD, (h + 1) * HD)
        grad = dot(kw[:, hc], dst[h], 0, 0)
        dq_ref[:, hc] = jnp.transpose(grad).astype(BF)

    for c in ys:
        c.wait_recv()
    total = s2[span(y, 16)].astype(F32)
    for d in range(NY - 1):
        total = total + yr[d].astype(F32)
    gy[span(y, 16)] = total.astype(BF)
    ys = []
    for d in range(1, NY):
        ys.append(send(gy.at[span(y, 16)], gy.at[span(y, 16)], ty, d - 1, y_peer(d)[1]))
    for c in ys:
        c.wait_recv()
    zs = []
    for d in range(1, NZ):
        zs.append(send(gy, gz.at[:, span(z, 128)], tz, d - 1, z_peer(d)[1]))
    gz[:, span(z, 128)] = gy[...]
    for c in zs:
        c.wait_recv()
    xs = []
    for d in range(1, NX):
        xs.append(send(gz, gx.at[span(x, 64)], tx, d - 1, x_peer(d)[1]))
    gx[span(x, 64)] = gz[...]

    rs2.wait_recv()
    out_ref[...] = (
        rs_keep[far] + rs_recv[far].astype(F32) + rs2_recv[...].astype(F32)
    ).astype(BF)
    for c in rets:
        c.wait_recv()
    for i, ref in ((0, dk_ref), (1, dv_ref)):
        ref[...] = (
            own_grad[i] + ret_recv[0, i].astype(F32) + ret_recv[1, i].astype(F32)
        ).astype(BF)
    for c in xs:
        c.wait_recv()
    dw_ref[...] = gx[...].astype(F32) * (NCTX * ROWS) ** (-0.5)
    for c in started:
        c.wait_send()


def shards(queries, keys, values, out_weight, grad_output, key_lists, key_counts):
    vmem = pl.BlockSpec(memory_space=pltpu.VMEM)
    smem = pl.BlockSpec(memory_space=pltpu.SMEM)
    dma = lambda n: pltpu.SemaphoreType.DMA((2, n))
    tok = jax.ShapeDtypeStruct(queries.shape, BF)
    return pl.pallas_call(
        layer_kernel,
        out_shape=(tok, tok, tok, tok, jax.ShapeDtypeStruct(out_weight.shape, F32)),
        in_specs=[vmem] * 6 + [smem],
        out_specs=[vmem] * 5,
        scratch_shapes=[
            pltpu.VMEM((WINDOW, 256), BF),
            pltpu.VMEM((WINDOW, 256), BF),
            pltpu.VMEM((16, ROWS), F32),
            pltpu.VMEM((HEADS_HERE, WINDOW, ROWS), F32),
            pltpu.VMEM((HEADS_HERE, WINDOW, ROWS), BF),
            pltpu.VMEM((HEADS_HERE, WINDOW, ROWS), BF),
            pltpu.VMEM((ROWS, 256), BF),
            pltpu.VMEM((ROWS, 256), BF),
            pltpu.VMEM((ROWS, 1024), BF),
            pltpu.VMEM((2, ROWS, 256), BF),
            pltpu.VMEM((2, ROWS, 256), BF),
            pltpu.VMEM((2, ROWS, 256), F32),
            pltpu.VMEM((ROWS, 256), BF),
            pltpu.VMEM((ROWS, 256), BF),
            pltpu.VMEM((2, 2, ROWS, 256), BF),
            pltpu.VMEM((2, 2, ROWS, 256), BF),
            pltpu.VMEM((2, ROWS, 256), F32),
            pltpu.VMEM((256, 1024), F32),
            pltpu.VMEM((256, 1024), BF),
            pltpu.VMEM((NX - 1, 64, 1024), BF),
            pltpu.VMEM((64, 1024), BF),
            pltpu.VMEM((NZ - 1, 64, 128), BF),
            pltpu.VMEM((64, 128), BF),
            pltpu.VMEM((NY - 1, 16, 128), BF),
            pltpu.VMEM((64, 128), BF),
            pltpu.VMEM((64, 1024), BF),
            pltpu.VMEM((256, 1024), BF),
            dma(4), dma(3), dma(3), dma(2),
            dma(NX - 1), dma(NZ - 1), dma(NY - 1), dma(NY - 1), dma(NZ - 1), dma(NX - 1),
        ],
        compiler_params=pltpu.CompilerParams(
            collective_id=0, has_side_effects=True, vmem_limit_bytes=62 * 1024 * 1024
        ),
        name="layer",
    )(queries, keys, values, out_weight, grad_output, key_lists, key_counts)


def solution(mesh):
    in_specs = (
        P("ctx", "head"),
        P("ctx", "head"),
        P("ctx", "head"),
        P("head", None),
        P("ctx", "head"),
        P(),
        P(),
    )
    out_specs = (
        P("ctx", "head"),
        P("ctx", "head"),
        P("ctx", "head"),
        P("ctx", "head"),
        P("head", None),
    )
    return jax.shard_map(shards, mesh=mesh, in_specs=in_specs, out_specs=out_specs, check_vma=False)
```

```python
import jax
import jax.numpy as jnp
from jax import lax
from jax.experimental import pallas as pl
from jax.experimental.pallas import tpu as pltpu
from jax.sharding import PartitionSpec as P

HD = 128
BLK = 128
MESH = pl.DeviceIdType.MESH
BF = jnp.bfloat16
F32 = jnp.float32
NY, NZ, NX = 4, 8, 4
NCTX = NY * NZ * NX
LOG2E = 1.4426950408889634
HEADS_HERE = 2
ROWS = 512
WINDOW = 3 * ROWS
CHUNK = 256


def dot(a, b, ca, cb):
    return lax.dot_general(a, b, (((ca,), (cb,)), ((), ())), preferred_element_type=F32)


def span(i, n):
    return pl.ds(pl.multiple_of(i * n, n), n)


def layer_kernel(
    q_ref, k_ref, v_ref, w_ref, g_ref, lists_ref, counts_ref,
    out_ref, dq_ref, dk_ref, dv_ref, dw_ref,
    kw, vw, bias, st, pt, dst, attn, ga, gfull,
    rs_send, rs_recv, rs_keep, rs2_send, rs2_recv,
    ret_send, ret_recv, own_grad, relay, relay2,
    part32, part, ax, as1, az, ay, agz, agx, bz, bs1, bx, by, bgx, bgz,
    halo_sem, head_sem, rs_sem, ret_sem, hop_sem, hop2_sem,
    sax, saz, say, taz, tax, sbz, sbx, sby, tbx, tbz,
):
    pos = lax.axis_index("ctx")
    hi = lax.axis_index("head")
    x = pos % NX
    z = (pos // NX) % NZ
    y = pos // (NX * NZ)
    core = hi % 2
    far = hi // 2

    def at(ctx, head):
        return {"ctx": ctx, "head": head}

    right = at((pos + 1) % NCTX, hi)
    left = at((pos + NCTX - 1) % NCTX, hi)
    mate = far * 2 + (1 - core)
    twin = (1 - far) * 2 + core
    to_mate = at(pos, mate)

    def y_hop(d):
        p = (far * NY + y + d) % (2 * NY)
        head = (p // NY) * 2 + core
        return head, at(((p % NY) * NZ + z) * NX + x, head)

    (up_head, up), (down_head, down) = y_hop(2), y_hop(6)

    def x_peer(d):
        p = (x + d) % NX
        return p, at((y * NZ + z) * NX + p, hi)

    def z_peer(d):
        p = (z + d) % NZ
        return p, at((y * NZ + p) * NX + x, hi)

    def y_peer(d):
        p = (y + d) % NY
        return p, at((p * NZ + z) * NX + x, hi)

    started = []

    def send(src, dst_, sems, k, device):
        c = pltpu.make_async_remote_copy(
            src_ref=src, dst_ref=dst_, send_sem=sems.at[0, k], recv_sem=sems.at[1, k],
            device_id=device, device_id_type=MESH,
        )
        c.start()
        started.append(c)
        return c

    barrier = pltpu.get_barrier_semaphore()
    peers = [right, left, to_mate, up, down]
    peers += [x_peer(d)[1] for d in range(1, NX)]
    peers += [z_peer(d)[1] for d in range(1, NZ)]
    peers += [y_peer(d)[1] for d in range(1, NY)]
    for device in peers:
        pl.semaphore_signal(barrier, inc=1, device_id=device, device_id_type=MESH)

    kw[ROWS : 2 * ROWS] = k_ref[...]
    vw[ROWS : 2 * ROWS] = v_ref[...]
    gfull[:, span(hi, 256)] = g_ref[...]
    pl.semaphore_wait(barrier, len(peers))

    halo = [
        send(k_ref, kw.at[0:ROWS], halo_sem, 0, right),
        send(k_ref, kw.at[2 * ROWS : 3 * ROWS], halo_sem, 1, left),
    ]
    quarter = lambda c: slice(c * BLK, (c + 1) * BLK)
    hops = [None] * 4
    for c in (0, 2, 1, 3):
        device = up if c < 2 else down
        hops[c] = send(g_ref.at[quarter(c)], relay.at[c], hop_sem, c, device)
    halo += [
        send(v_ref, vw.at[0:ROWS], halo_sem, 2, right),
        send(v_ref, vw.at[2 * ROWS : 3 * ROWS], halo_sem, 3, left),
    ]
    g_mate = send(g_ref, gfull.at[:, span(hi, 256)], head_sem, 1, to_mate)

    g_far = []
    rs2 = []

    def pass_on(c):
        hops[c].wait_recv()
        device, head = (up, down_head) if c < 2 else (down, up_head)
        g_far.append(
            send(relay.at[c], gfull.at[quarter(c), span(head, 256)], hop_sem, 4 + c, device)
        )

    tile = lists_ref[:, span(pos // 32, 128)].astype(F32)
    slot = lax.broadcasted_iota(jnp.int32, (8, BLK), 0)
    lane = lax.broadcasted_iota(jnp.int32, (8, BLK), 1)
    for n in range(4):
        row = jnp.max(
            jnp.where(lane == (pos % 32) * 4 + n, tile, -1.0), axis=1, keepdims=True
        )
        row = jnp.where(slot < counts_ref[pos * 4 + n], jnp.broadcast_to(row, (8, BLK)), -1.0)
        for wb in range(12):
            block = ((pos + NCTX - 1) * 4 + wb) % (NCTX * 4)
            hit = jnp.where(row == block.astype(F32), 1.0, 0.0)
            hit = jnp.max(hit, axis=0, keepdims=True)
            bias[wb : wb + 1, n * BLK : (n + 1) * BLK] = jnp.where(hit > 0.5, 0.0, -jnp.inf)

    factor = HD ** (-0.5)

    def score_chunk(h, c):
        hc = slice(h * HD, (h + 1) * HD)
        s = dot(kw[c * CHUNK : (c + 1) * CHUNK, hc], q_ref[:, hc], 1, 1) * (factor * LOG2E)
        for b in range(CHUNK // BLK):
            wb = c * (CHUNK // BLK) + b
            st[h, wb * BLK : (wb + 1) * BLK] = s[b * BLK : (b + 1) * BLK] + bias[wb : wb + 1]

    for h in range(HEADS_HERE):
        for c in (2, 3):
            score_chunk(h, c)
    pass_on(0)
    pass_on(2)
    halo[0].wait_recv()
    for h in range(HEADS_HERE):
        for c in (0, 1):
            score_chunk(h, c)
    pass_on(1)
    pass_on(3)
    halo[1].wait_recv()
    for h in range(HEADS_HERE):
        for c in (4, 5):
            score_chunk(h, c)
    for h in range(HEADS_HERE):
        top = jnp.max(st[h], axis=0, keepdims=True)
        total = jnp.zeros((1, ROWS), F32)
        for c in range(WINDOW // CHUNK):
            keys = slice(c * CHUNK, (c + 1) * CHUNK)
            e = jnp.exp2(st[h, keys] - top)
            st[h, keys] = e
            total = total + jnp.sum(e, axis=0, keepdims=True)
        inverse = 1.0 / total
        for c in range(WINDOW // CHUNK):
            keys = slice(c * CHUNK, (c + 1) * CHUNK)
            pt[h, keys] = (st[h, keys] * inverse).astype(BF)
    halo[2].wait_recv()
    halo[3].wait_recv()
    attn_t = []
    for h in range(HEADS_HERE):
        hc = slice(h * HD, (h + 1) * HD)
        mixed = dot(vw[:, hc], pt[h], 0, 0)
        attn_t.append(mixed.astype(BF))
        attn[:, hc] = jnp.transpose(mixed).astype(BF)

    g_share = []
    for c, got in zip((0, 2, 1, 3), g_far):
        got.wait_recv()
        view = gfull.at[quarter(c), span(twin, 256)]
        g_share.append(send(view, view, head_sem, 2 + c, to_mate))
    for f in range(2):
        cols = span(f * 2 + (1 - core), 256)
        rs_send[f] = dot(attn[...], w_ref[:, cols], 1, 0).astype(BF)
    rs = [send(rs_send.at[f], rs_recv.at[f], rs_sem, f, to_mate) for f in range(2)]
    for f in range(2):
        cols = span(f * 2 + core, 256)
        rs_keep[f] = dot(attn[...], w_ref[:, cols], 1, 0)
    g_mate.wait_recv()
    for c in g_share:
        c.wait_recv()

    for h in range(HEADS_HERE):
        value = dot(attn_t[h], gfull[...], 1, 0)
        part32[h * HD : (h + 1) * HD] = value
        part[h * HD : (h + 1) * HD] = value.astype(BF)
    cut = 4 * HD
    a_x, b_z = [], []
    for d in range(1, NX):
        p, device = x_peer(d)
        a_x.append(send(part.at[:, span(p, 128)], ax.at[d - 1], sax, d - 1, device))
    for d in range(1, NZ):
        p, device = z_peer(d)
        b_z.append(send(part.at[span(p, 32), cut:], bz.at[d - 1], sbz, d - 1, device))

    row_dots = []
    for h in range(HEADS_HERE):
        hc = slice(h * HD, (h + 1) * HD)
        back = dot(w_ref[hc], gfull[...], 1, 1).astype(BF).astype(F32)
        row_dots.append(jnp.sum(back * attn_t[h].astype(F32), axis=0, keepdims=True))
        ga[:, hc] = jnp.transpose(back).astype(BF)

    for c in rs:
        c.wait_recv()
    rs2_send[...] = (rs_keep[1 - far] + rs_recv[1 - far].astype(F32)).astype(BF)
    hops2 = [None] * 4
    for c in (0, 2, 1, 3):
        device = up if c < 2 else down
        hops2[c] = send(rs2_send.at[quarter(c)], relay2.at[c], hop2_sem, c, device)

    def pass_on2(c):
        hops2[c].wait_recv()
        rs2.append(
            send(relay2.at[c], rs2_recv.at[quarter(c)], hop2_sem, 4 + c, up if c < 2 else down)
        )

    def back_chunk(h, c):
        hc = slice(h * HD, (h + 1) * HD)
        keys = slice(c * CHUNK, (c + 1) * CHUNK)
        dp = dot(vw[keys, hc], ga[:, hc], 1, 1)
        ds = pt[h, keys].astype(F32) * ((dp - row_dots[h]) * factor)
        dst[h, keys] = ds.astype(BF)

    def key_grads(h, side):
        hc = slice(h * HD, (h + 1) * HD)
        keys = slice(side * ROWS, (side + 1) * ROWS)
        return dot(dst[h, keys], q_ref[:, hc], 1, 0), dot(pt[h, keys], ga[:, hc], 1, 0)

    rets = []
    for i, side, device in ((0, 2, right), (1, 0, left)):
        for h in range(HEADS_HERE):
            hc = slice(h * HD, (h + 1) * HD)
            for c in (side * 2, side * 2 + 1):
                back_chunk(h, c)
            dk, dv = key_grads(h, side)
            ret_send[i, 0, :, hc] = dk.astype(BF)
            ret_send[i, 1, :, hc] = dv.astype(BF)
        rets.append(send(ret_send.at[i], ret_recv.at[i], ret_sem, i, device))

    def total_of(first, copies, slots):
        value = first.astype(F32)
        for i, c in enumerate(copies):
            c.wait_recv()
            value = value + slots[i].astype(F32)
        return value.astype(BF)

    as1[...] = total_of(part32[:, span(x, 128)], a_x, ax)
    a_z = []
    for d in range(1, NZ):
        p, device = z_peer(d)
        a_z.append(send(as1.at[span(p, 32)], az.at[d - 1], saz, d - 1, device))
    bs1[...] = total_of(part32[span(z, 32), cut:], b_z, bz)
    b_x = []
    for d in range(1, NX):
        p, device = x_peer(d)
        b_x.append(send(bs1.at[:, span(p, 128)], bx.at[d - 1], sbx, d - 1, device))
    pass_on2(0)
    pass_on2(2)

    for h in range(HEADS_HERE):
        hc = slice(h * HD, (h + 1) * HD)
        for c in (2, 3):
            back_chunk(h, c)
        dk, dv = key_grads(h, 1)
        own_grad[0, :, hc] = dk
        own_grad[1, :, hc] = dv

    ay[y] = total_of(as1[span(z, 32)], a_z, az)
    a_y = [send(ay.at[y], ay.at[y], say, d - 1, y_peer(d)[1]) for d in range(1, NY)]
    by[y] = total_of(bs1[:, span(x, 128)], b_x, bx)
    b_y = [send(by.at[y], by.at[y], sby, d - 1, y_peer(d)[1]) for d in range(1, NY)]
    pass_on2(1)
    pass_on2(3)

    for h in range(HEADS_HERE):
        hc = slice(h * HD, (h + 1) * HD)
        grad = dot(kw[:, hc], dst[h], 0, 0)
        dq_ref[:, hc] = jnp.transpose(grad).astype(BF)

    def y_total(copies, slots):
        for c in copies:
            c.wait_recv()
        value = slots[0].astype(F32)
        for i in range(1, NY):
            value = value + slots[i].astype(F32)
        return value.astype(BF)

    agz[span(z, 32)] = y_total(a_y, ay)
    view = agz.at[span(z, 32)]
    a_gz = [send(view, view, taz, d - 1, z_peer(d)[1]) for d in range(1, NZ)]
    bgx[:, span(x, 128)] = y_total(b_y, by)
    view_b = bgx.at[:, span(x, 128)]
    b_gx = [send(view_b, view_b, tbx, d - 1, x_peer(d)[1]) for d in range(1, NX)]
    for c in b_gx:
        c.wait_recv()
    b_gz = [send(bgx, bgz.at[span(z, 32)], tbz, d - 1, z_peer(d)[1]) for d in range(1, NZ)]
    bgz[span(z, 32)] = bgx[...]
    for c in a_gz:
        c.wait_recv()
    a_gx = [send(agz, agx.at[:, span(x, 128)], tax, d - 1, x_peer(d)[1]) for d in range(1, NX)]
    agx[:, span(x, 128)] = agz[...]

    for c in rs2:
        c.wait_recv()
    out_ref[...] = (
        rs_keep[far] + rs_recv[far].astype(F32) + rs2_recv[...].astype(F32)
    ).astype(BF)
    for c in rets:
        c.wait_recv()
    for i, ref in ((0, dk_ref), (1, dv_ref)):
        ref[...] = (
            own_grad[i] + ret_recv[0, i].astype(F32) + ret_recv[1, i].astype(F32)
        ).astype(BF)
    scale = (NCTX * ROWS) ** (-0.5)
    for c in b_gz:
        c.wait_recv()
    dw_ref[:, cut:] = bgz[...].astype(F32) * scale
    for c in a_gx:
        c.wait_recv()
    dw_ref[:, :cut] = agx[...].astype(F32) * scale
    for c in started:
        c.wait_send()


def hand_out_kernel(*refs):
    n = len(refs) // 3
    sources, targets, held = refs[:n], refs[n : 2 * n], refs[2 * n : 3 * n]
    sem = refs[3 * n]
    reads = [pltpu.make_async_copy(sources[i], held[i], sem.at[0, i]) for i in range(n)]
    writes = [pltpu.make_async_copy(held[i], targets[i], sem.at[1, i]) for i in range(n)]
    for c in reads:
        c.start()
    for i in range(n):
        reads[i].wait()
        writes[i].start()
    for c in writes:
        c.wait()


def hand_out(arrays):
    shapes = [jax.ShapeDtypeStruct(a.shape, a.dtype) for a in arrays]
    n = len(arrays)
    hbm = pl.BlockSpec(memory_space=pl.ANY)
    return pl.pallas_call(
        hand_out_kernel,
        out_shape=shapes,
        in_specs=[hbm] * n,
        out_specs=[hbm] * n,
        scratch_shapes=[pltpu.VMEM(a.shape, a.dtype) for a in arrays]
        + [pltpu.SemaphoreType.DMA((2, n))],
        name="hand_out",
    )(*arrays)


def shards(queries, keys, values, out_weight, grad_output, key_lists, key_counts):
    vmem = pl.BlockSpec(memory_space=pltpu.VMEM)
    smem = pl.BlockSpec(memory_space=pltpu.SMEM)
    dma = lambda n: pltpu.SemaphoreType.DMA((2, n))
    tok = jax.ShapeDtypeStruct(queries.shape, BF)
    results = pl.pallas_call(
        layer_kernel,
        out_shape=(tok, tok, tok, tok, jax.ShapeDtypeStruct(out_weight.shape, F32)),
        in_specs=[vmem] * 6 + [smem],
        out_specs=[vmem] * 5,
        scratch_shapes=[
            pltpu.VMEM((WINDOW, 256), BF),
            pltpu.VMEM((WINDOW, 256), BF),
            pltpu.VMEM((16, ROWS), F32),
            pltpu.VMEM((HEADS_HERE, WINDOW, ROWS), F32),
            pltpu.VMEM((HEADS_HERE, WINDOW, ROWS), BF),
            pltpu.VMEM((HEADS_HERE, WINDOW, ROWS), BF),
            pltpu.VMEM((ROWS, 256), BF),
            pltpu.VMEM((ROWS, 256), BF),
            pltpu.VMEM((ROWS, 1024), BF),
            pltpu.VMEM((2, ROWS, 256), BF),
            pltpu.VMEM((2, ROWS, 256), BF),
            pltpu.VMEM((2, ROWS, 256), F32),
            pltpu.VMEM((ROWS, 256), BF),
            pltpu.VMEM((ROWS, 256), BF),
            pltpu.VMEM((2, 2, ROWS, 256), BF),
            pltpu.VMEM((2, 2, ROWS, 256), BF),
            pltpu.VMEM((2, ROWS, 256), F32),
            pltpu.VMEM((4, BLK, 256), BF),
            pltpu.VMEM((4, BLK, 256), BF),
            pltpu.VMEM((256, 1024), F32),
            pltpu.VMEM((256, 1024), BF),
            pltpu.VMEM((NX - 1, 256, 128), BF),
            pltpu.VMEM((256, 128), BF),
            pltpu.VMEM((NZ - 1, 32, 128), BF),
            pltpu.VMEM((NY, 32, 128), BF),
            pltpu.VMEM((256, 128), BF),
            pltpu.VMEM((256, 512), BF),
            pltpu.VMEM((NZ - 1, 32, 512), BF),
            pltpu.VMEM((32, 512), BF),
            pltpu.VMEM((NX - 1, 32, 128), BF),
            pltpu.VMEM((NY, 32, 128), BF),
            pltpu.VMEM((32, 512), BF),
            pltpu.VMEM((256, 512), BF),
            dma(4), dma(6), dma(2), dma(2), dma(8), dma(8),
            dma(NX - 1), dma(NZ - 1), dma(NY - 1), dma(NZ - 1), dma(NX - 1),
            dma(NZ - 1), dma(NX - 1), dma(NY - 1), dma(NX - 1), dma(NZ - 1),
        ],
        compiler_params=pltpu.CompilerParams(
            collective_id=0, has_side_effects=True, vmem_limit_bytes=62 * 1024 * 1024
        ),
        name="layer",
    )(queries, keys, values, out_weight, grad_output, key_lists.T, key_counts)
    return hand_out(results)


def solution(mesh):
    in_specs = (
        P("ctx", "head"),
        P("ctx", "head"),
        P("ctx", "head"),
        P("head", None),
        P("ctx", "head"),
        P(),
        P(),
    )
    out_specs = (
        P("ctx", "head"),
        P("ctx", "head"),
        P("ctx", "head"),
        P("ctx", "head"),
        P("head", None),
    )
    return jax.shard_map(shards, mesh=mesh, in_specs=in_specs, out_specs=out_specs, check_vma=False)
```

```python
import jax
import jax.numpy as jnp
from jax import lax
from jax.experimental import pallas as pl
from jax.experimental.pallas import tpu as pltpu
from jax.sharding import PartitionSpec as P

HD = 128
BLK = 128
MESH = pl.DeviceIdType.MESH
BF = jnp.bfloat16
F32 = jnp.float32
NY, NZ, NX = 4, 8, 4
NCTX = NY * NZ * NX
LOG2E = 1.4426950408889634
HEADS_HERE = 2
ROWS = 512
WINDOW = 3 * ROWS
CHUNK = 256


def dot(a, b, ca, cb):
    return lax.dot_general(a, b, (((ca,), (cb,)), ((), ())), preferred_element_type=F32)


def span(i, n):
    return pl.ds(pl.multiple_of(i * n, n), n)


def layer_kernel(
    q_hbm, k_hbm, v_hbm, w_hbm, g_hbm, lists_ref, counts_ref,
    out_ref, dq_ref, dk_ref, dv_ref, dw_ref,
    q_ref, w_ref,
    kw, vw, bias, st, pt, dst, attn, ga, gfull,
    rs_send, rs_recv, rs_keep, rs2_send, rs2_recv,
    ret_send, ret_recv, own_grad, relay, relay2,
    part32, part, ax, as1, az, ay, agz, agx, bz, bs1, bx, by, bgx, bgz,
    load_sem, halo_sem, head_sem, rs_sem, ret_sem, hop_sem, hop2_sem,
    sax, saz, say, taz, tax, sbz, sbx, sby, tbx, tbz,
):
    pos = lax.axis_index("ctx")
    hi = lax.axis_index("head")
    x = pos % NX
    z = (pos // NX) % NZ
    y = pos // (NX * NZ)
    core = hi % 2
    far = hi // 2

    def at(ctx, head):
        return {"ctx": ctx, "head": head}

    right = at((pos + 1) % NCTX, hi)
    left = at((pos + NCTX - 1) % NCTX, hi)
    mate = far * 2 + (1 - core)
    twin = (1 - far) * 2 + core
    to_mate = at(pos, mate)

    def y_hop(d):
        p = (far * NY + y + d) % (2 * NY)
        head = (p // NY) * 2 + core
        return head, at(((p % NY) * NZ + z) * NX + x, head)

    (up_head, up), (down_head, down) = y_hop(2), y_hop(6)

    def x_peer(d):
        p = (x + d) % NX
        return p, at((y * NZ + z) * NX + p, hi)

    def z_peer(d):
        p = (z + d) % NZ
        return p, at((y * NZ + p) * NX + x, hi)

    def y_peer(d):
        p = (y + d) % NY
        return p, at((p * NZ + z) * NX + x, hi)

    started = []

    def send(src, dst_, sems, k, device):
        c = pltpu.make_async_remote_copy(
            src_ref=src, dst_ref=dst_, send_sem=sems.at[0, k], recv_sem=sems.at[1, k],
            device_id=device, device_id_type=MESH,
        )
        c.start()
        started.append(c)
        return c

    k_ref, v_ref = kw.at[ROWS : 2 * ROWS], vw.at[ROWS : 2 * ROWS]
    g_ref = gfull.at[:, span(hi, 256)]
    barrier = pltpu.get_barrier_semaphore()
    peers = [right, left, to_mate, up, down]
    peers += [x_peer(d)[1] for d in range(1, NX)]
    peers += [z_peer(d)[1] for d in range(1, NZ)]
    peers += [y_peer(d)[1] for d in range(1, NY)]
    for device in peers:
        pl.semaphore_signal(barrier, inc=1, device_id=device, device_id_type=MESH)
    pairs = ((k_hbm, k_ref), (v_hbm, v_ref), (g_hbm, g_ref), (q_hbm, q_ref), (w_hbm, w_ref))
    loads = [
        pltpu.make_async_copy(a, b, load_sem.at[i]) for i, (a, b) in enumerate(pairs)
    ]
    for c in loads:
        c.start()
    for c in loads:
        c.wait()
    pl.semaphore_wait(barrier, len(peers))

    halo = [
        send(k_ref, kw.at[0:ROWS], halo_sem, 0, right),
        send(k_ref, kw.at[2 * ROWS : 3 * ROWS], halo_sem, 1, left),
    ]
    quarter = lambda c: slice(c * BLK, (c + 1) * BLK)
    hops = [None] * 4
    for c in (0, 2, 1, 3):
        device = up if c < 2 else down
        hops[c] = send(g_ref.at[quarter(c)], relay.at[c], hop_sem, c, device)
    halo += [
        send(v_ref, vw.at[0:ROWS], halo_sem, 2, right),
        send(v_ref, vw.at[2 * ROWS : 3 * ROWS], halo_sem, 3, left),
    ]
    g_mate = send(g_ref, gfull.at[:, span(hi, 256)], head_sem, 1, to_mate)

    g_far = []
    rs2 = []

    def pass_on(c):
        hops[c].wait_recv()
        device, head = (up, down_head) if c < 2 else (down, up_head)
        g_far.append(
            send(relay.at[c], gfull.at[quarter(c), span(head, 256)], hop_sem, 4 + c, device)
        )

    tile = lists_ref[:, span(pos // 32, 128)].astype(F32)
    slot = lax.broadcasted_iota(jnp.int32, (8, BLK), 0)
    lane = lax.broadcasted_iota(jnp.int32, (8, BLK), 1)
    for n in range(4):
        row = jnp.max(
            jnp.where(lane == (pos % 32) * 4 + n, tile, -1.0), axis=1, keepdims=True
        )
        row = jnp.where(slot < counts_ref[pos * 4 + n], jnp.broadcast_to(row, (8, BLK)), -1.0)
        for wb in range(12):
            block = ((pos + NCTX - 1) * 4 + wb) % (NCTX * 4)
            hit = jnp.where(row == block.astype(F32), 1.0, 0.0)
            hit = jnp.max(hit, axis=0, keepdims=True)
            bias[wb : wb + 1, n * BLK : (n + 1) * BLK] = jnp.where(hit > 0.5, 0.0, -jnp.inf)

    factor = HD ** (-0.5)

    def score_chunk(h, c):
        hc = slice(h * HD, (h + 1) * HD)
        s = dot(kw[c * CHUNK : (c + 1) * CHUNK, hc], q_ref[:, hc], 1, 1) * (factor * LOG2E)
        for b in range(CHUNK // BLK):
            wb = c * (CHUNK // BLK) + b
            st[h, wb * BLK : (wb + 1) * BLK] = s[b * BLK : (b + 1) * BLK] + bias[wb : wb + 1]

    for h in range(HEADS_HERE):
        for c in (2, 3):
            score_chunk(h, c)
    pass_on(0)
    pass_on(2)
    halo[0].wait_recv()
    for h in range(HEADS_HERE):
        for c in (0, 1):
            score_chunk(h, c)
    pass_on(1)
    pass_on(3)
    halo[1].wait_recv()
    for h in range(HEADS_HERE):
        for c in (4, 5):
            score_chunk(h, c)
    for h in range(HEADS_HERE):
        top = jnp.max(st[h], axis=0, keepdims=True)
        total = jnp.zeros((1, ROWS), F32)
        for c in range(WINDOW // CHUNK):
            keys = slice(c * CHUNK, (c + 1) * CHUNK)
            e = jnp.exp2(st[h, keys] - top)
            st[h, keys] = e
            total = total + jnp.sum(e, axis=0, keepdims=True)
        inverse = 1.0 / total
        for c in range(WINDOW // CHUNK):
            keys = slice(c * CHUNK, (c + 1) * CHUNK)
            pt[h, keys] = (st[h, keys] * inverse).astype(BF)
    halo[2].wait_recv()
    halo[3].wait_recv()
    attn_t = []
    for h in range(HEADS_HERE):
        hc = slice(h * HD, (h + 1) * HD)
        mixed = dot(vw[:, hc], pt[h], 0, 0)
        attn_t.append(mixed.astype(BF))
        attn[:, hc] = jnp.transpose(mixed).astype(BF)

    g_share = []
    for c, got in zip((0, 2, 1, 3), g_far):
        got.wait_recv()
        view = gfull.at[quarter(c), span(twin, 256)]
        g_share.append(send(view, view, head_sem, 2 + c, to_mate))
    for f in range(2):
        cols = span(f * 2 + (1 - core), 256)
        rs_send[f] = dot(attn[...], w_ref[:, cols], 1, 0).astype(BF)
    rs = [send(rs_send.at[f], rs_recv.at[f], rs_sem, f, to_mate) for f in range(2)]
    for f in range(2):
        cols = span(f * 2 + core, 256)
        rs_keep[f] = dot(attn[...], w_ref[:, cols], 1, 0)
    g_mate.wait_recv()
    for c in g_share:
        c.wait_recv()

    for h in range(HEADS_HERE):
        value = dot(attn_t[h], gfull[...], 1, 0)
        part32[h * HD : (h + 1) * HD] = value
        part[h * HD : (h + 1) * HD] = value.astype(BF)
    cut = 4 * HD
    a_x, b_z = [], []
    for d in range(1, NX):
        p, device = x_peer(d)
        a_x.append(send(part.at[:, span(p, 128)], ax.at[d - 1], sax, d - 1, device))
    for d in range(1, NZ):
        p, device = z_peer(d)
        b_z.append(send(part.at[span(p, 32), cut:], bz.at[d - 1], sbz, d - 1, device))

    row_dots = []
    for h in range(HEADS_HERE):
        hc = slice(h * HD, (h + 1) * HD)
        back = dot(w_ref[hc], gfull[...], 1, 1).astype(BF).astype(F32)
        row_dots.append(jnp.sum(back * attn_t[h].astype(F32), axis=0, keepdims=True))
        ga[:, hc] = jnp.transpose(back).astype(BF)

    for c in rs:
        c.wait_recv()
    rs2_send[...] = (rs_keep[1 - far] + rs_recv[1 - far].astype(F32)).astype(BF)
    hops2 = [None] * 4
    for c in (0, 2, 1, 3):
        device = up if c < 2 else down
        hops2[c] = send(rs2_send.at[quarter(c)], relay2.at[c], hop2_sem, c, device)

    def pass_on2(c):
        hops2[c].wait_recv()
        rs2.append(
            send(relay2.at[c], rs2_recv.at[quarter(c)], hop2_sem, 4 + c, up if c < 2 else down)
        )

    def back_chunk(h, c):
        hc = slice(h * HD, (h + 1) * HD)
        keys = slice(c * CHUNK, (c + 1) * CHUNK)
        dp = dot(vw[keys, hc], ga[:, hc], 1, 1)
        ds = pt[h, keys].astype(F32) * ((dp - row_dots[h]) * factor)
        dst[h, keys] = ds.astype(BF)

    def key_grads(h, side):
        hc = slice(h * HD, (h + 1) * HD)
        keys = slice(side * ROWS, (side + 1) * ROWS)
        return dot(dst[h, keys], q_ref[:, hc], 1, 0), dot(pt[h, keys], ga[:, hc], 1, 0)

    rets = []
    for i, side, device in ((0, 2, right), (1, 0, left)):
        for h in range(HEADS_HERE):
            hc = slice(h * HD, (h + 1) * HD)
            for c in (side * 2, side * 2 + 1):
                back_chunk(h, c)
            dk, dv = key_grads(h, side)
            ret_send[i, 0, :, hc] = dk.astype(BF)
            ret_send[i, 1, :, hc] = dv.astype(BF)
        rets.append(send(ret_send.at[i, 0], ret_recv.at[i, 0], ret_sem, i, device))

    def total_of(first, copies, slots):
        value = first.astype(F32)
        for i, c in enumerate(copies):
            c.wait_recv()
            value = value + slots[i].astype(F32)
        return value.astype(BF)

    as1[...] = total_of(part32[:, span(x, 128)], a_x, ax)
    a_z = []
    for d in range(1, NZ):
        p, device = z_peer(d)
        a_z.append(send(as1.at[span(p, 32)], az.at[d - 1], saz, d - 1, device))
    bs1[...] = total_of(part32[span(z, 32), cut:], b_z, bz)
    b_x = []
    for d in range(1, NX):
        p, device = x_peer(d)
        b_x.append(send(bs1.at[:, span(p, 128)], bx.at[d - 1], sbx, d - 1, device))
    for i, device in ((0, right), (1, left)):
        rets.append(send(ret_send.at[i, 1], ret_recv.at[i, 1], ret_sem, 2 + i, device))
    pass_on2(0)
    pass_on2(2)

    for h in range(HEADS_HERE):
        hc = slice(h * HD, (h + 1) * HD)
        for c in (2, 3):
            back_chunk(h, c)
        dk, dv = key_grads(h, 1)
        own_grad[0, :, hc] = dk
        own_grad[1, :, hc] = dv

    ay[y] = total_of(as1[span(z, 32)], a_z, az)
    a_y = [send(ay.at[y], ay.at[y], say, d - 1, y_peer(d)[1]) for d in range(1, NY)]
    by[y] = total_of(bs1[:, span(x, 128)], b_x, bx)
    b_y = [send(by.at[y], by.at[y], sby, d - 1, y_peer(d)[1]) for d in range(1, NY)]
    pass_on2(1)
    pass_on2(3)

    for h in range(HEADS_HERE):
        hc = slice(h * HD, (h + 1) * HD)
        grad = dot(kw[:, hc], dst[h], 0, 0)
        dq_ref[:, hc] = jnp.transpose(grad).astype(BF)

    def y_total(copies, slots):
        for c in copies:
            c.wait_recv()
        value = slots[0].astype(F32)
        for i in range(1, NY):
            value = value + slots[i].astype(F32)
        return value.astype(BF)

    agz[span(z, 32)] = y_total(a_y, ay)
    view = agz.at[span(z, 32)]
    a_gz = [send(view, view, taz, d - 1, z_peer(d)[1]) for d in range(1, NZ)]
    a_gx, b_gz = [], []

    def a_on(e):
        rows = span((z + NZ - e) % NZ, 32)
        for d in range(1, NX):
            to = agx.at[rows, span(x, 128)]
            a_gx.append(send(agz.at[rows], to, tax, e * (NX - 1) + d - 1, x_peer(d)[1]))

    def b_on(e):
        cols = span((x + NX - e) % NX, 128)
        for d in (4, 3, 5, 2, 6, 1, 7):
            to = bgz.at[span(z, 32), cols]
            b_gz.append(send(bgx.at[:, cols], to, tbz, e * (NZ - 1) + d - 1, z_peer(d)[1]))

    bgx[:, span(x, 128)] = y_total(b_y, by)
    view_b = bgx.at[:, span(x, 128)]
    b_gx = [send(view_b, view_b, tbx, d - 1, x_peer(d)[1]) for d in range(1, NX)]
    b_on(0)
    a_on(0)
    for e in (1, 3, 2):
        b_gx[e - 1].wait_recv()
        b_on(e)
    bgz[span(z, 32)] = bgx[...]
    for e in (1, 7, 2, 6, 3, 5, 4):
        a_gz[e - 1].wait_recv()
        a_on(e)
    agx[:, span(x, 128)] = agz[...]

    for c in rs2:
        c.wait_recv()
    out_ref[...] = (
        rs_keep[far] + rs_recv[far].astype(F32) + rs2_recv[...].astype(F32)
    ).astype(BF)
    for c in rets:
        c.wait_recv()
    for i, ref in ((0, dk_ref), (1, dv_ref)):
        ref[...] = (
            own_grad[i] + ret_recv[0, i].astype(F32) + ret_recv[1, i].astype(F32)
        ).astype(BF)
    scale = (NCTX * ROWS) ** (-0.5)
    for c in b_gz:
        c.wait_recv()
    dw_ref[:, cut:] = bgz[...].astype(F32) * scale
    for c in a_gx:
        c.wait_recv()
    dw_ref[:, :cut] = agx[...].astype(F32) * scale
    for c in started:
        c.wait_send()


def hand_out_kernel(*refs):
    n = len(refs) // 3
    sources, targets, held = refs[:n], refs[n : 2 * n], refs[2 * n : 3 * n]
    sem = refs[3 * n]
    reads = [pltpu.make_async_copy(sources[i], held[i], sem.at[0, i]) for i in range(n)]
    writes = [pltpu.make_async_copy(held[i], targets[i], sem.at[1, i]) for i in range(n)]
    for c in reads:
        c.start()
    for i in range(n):
        reads[i].wait()
        writes[i].start()
    for c in writes:
        c.wait()


def hand_out(arrays):
    shapes = [jax.ShapeDtypeStruct(a.shape, a.dtype) for a in arrays]
    n = len(arrays)
    hbm = pl.BlockSpec(memory_space=pl.ANY)
    return pl.pallas_call(
        hand_out_kernel,
        out_shape=shapes,
        in_specs=[hbm] * n,
        out_specs=[hbm] * n,
        scratch_shapes=[pltpu.VMEM(a.shape, a.dtype) for a in arrays]
        + [pltpu.SemaphoreType.DMA((2, n))],
        name="hand_out",
    )(*arrays)


def shards(queries, keys, values, out_weight, grad_output, key_lists, key_counts):
    vmem = pl.BlockSpec(memory_space=pltpu.VMEM)
    smem = pl.BlockSpec(memory_space=pltpu.SMEM)
    dma = lambda n: pltpu.SemaphoreType.DMA((2, n))
    tok = jax.ShapeDtypeStruct(queries.shape, BF)
    results = pl.pallas_call(
        layer_kernel,
        out_shape=(tok, tok, tok, tok, jax.ShapeDtypeStruct(out_weight.shape, F32)),
        in_specs=[pl.BlockSpec(memory_space=pl.ANY)] * 5 + [vmem, smem],
        out_specs=[vmem] * 5,
        scratch_shapes=[
            pltpu.VMEM((ROWS, 256), BF),
            pltpu.VMEM((256, 1024), BF),
            pltpu.VMEM((WINDOW, 256), BF),
            pltpu.VMEM((WINDOW, 256), BF),
            pltpu.VMEM((16, ROWS), F32),
            pltpu.VMEM((HEADS_HERE, WINDOW, ROWS), F32),
            pltpu.VMEM((HEADS_HERE, WINDOW, ROWS), BF),
            pltpu.VMEM((HEADS_HERE, WINDOW, ROWS), BF),
            pltpu.VMEM((ROWS, 256), BF),
            pltpu.VMEM((ROWS, 256), BF),
            pltpu.VMEM((ROWS, 1024), BF),
            pltpu.VMEM((2, ROWS, 256), BF),
            pltpu.VMEM((2, ROWS, 256), BF),
            pltpu.VMEM((2, ROWS, 256), F32),
            pltpu.VMEM((ROWS, 256), BF),
            pltpu.VMEM((ROWS, 256), BF),
            pltpu.VMEM((2, 2, ROWS, 256), BF),
            pltpu.VMEM((2, 2, ROWS, 256), BF),
            pltpu.VMEM((2, ROWS, 256), F32),
            pltpu.VMEM((4, BLK, 256), BF),
            pltpu.VMEM((4, BLK, 256), BF),
            pltpu.VMEM((256, 1024), F32),
            pltpu.VMEM((256, 1024), BF),
            pltpu.VMEM((NX - 1, 256, 128), BF),
            pltpu.VMEM((256, 128), BF),
            pltpu.VMEM((NZ - 1, 32, 128), BF),
            pltpu.VMEM((NY, 32, 128), BF),
            pltpu.VMEM((256, 128), BF),
            pltpu.VMEM((256, 512), BF),
            pltpu.VMEM((NZ - 1, 32, 512), BF),
            pltpu.VMEM((32, 512), BF),
            pltpu.VMEM((NX - 1, 32, 128), BF),
            pltpu.VMEM((NY, 32, 128), BF),
            pltpu.VMEM((32, 512), BF),
            pltpu.VMEM((256, 512), BF),
            pltpu.SemaphoreType.DMA((5,)), dma(4), dma(6), dma(2), dma(4), dma(8), dma(8),
            dma(NX - 1), dma(NZ - 1), dma(NY - 1), dma(NZ - 1), dma(NZ * (NX - 1)),
            dma(NZ - 1), dma(NX - 1), dma(NY - 1), dma(NX - 1), dma(NX * (NZ - 1)),
        ],
        compiler_params=pltpu.CompilerParams(
            collective_id=0, has_side_effects=True, vmem_limit_bytes=62 * 1024 * 1024
        ),
        name="layer",
    )(queries, keys, values, out_weight, grad_output, key_lists.T, key_counts)
    return hand_out(results)


def solution(mesh):
    in_specs = (
        P("ctx", "head"),
        P("ctx", "head"),
        P("ctx", "head"),
        P("head", None),
        P("ctx", "head"),
        P(),
        P(),
    )
    out_specs = (
        P("ctx", "head"),
        P("ctx", "head"),
        P("ctx", "head"),
        P("ctx", "head"),
        P("head", None),
    )
    return jax.shard_map(shards, mesh=mesh, in_specs=in_specs, out_specs=out_specs, check_vma=False)
```

```python
import jax
import jax.numpy as jnp
from jax import lax
from jax.experimental import pallas as pl
from jax.experimental.pallas import tpu as pltpu
from jax.sharding import PartitionSpec as P

HD = 128
BLK = 128
MESH = pl.DeviceIdType.MESH
BF = jnp.bfloat16
F32 = jnp.float32
NY, NZ, NX = 4, 8, 4
NCTX = NY * NZ * NX
LOG2E = 1.4426950408889634
HEADS_HERE = 2
ROWS = 512
WINDOW = 3 * ROWS
CHUNK = 256


def dot(a, b, ca, cb):
    return lax.dot_general(a, b, (((ca,), (cb,)), ((), ())), preferred_element_type=F32)


def span(i, n):
    return pl.ds(pl.multiple_of(i * n, n), n)


def layer_kernel(
    q_hbm, k_hbm, v_hbm, w_hbm, g_hbm, lists_ref, counts_ref,
    out_ref, dq_ref, dk_ref, dv_ref, dw_ref,
    q_ref, w_ref,
    kw, vw, bias, st, pt, dst, attn, ga, gfull,
    rs_send, rs_recv, rs_keep, rs2_send, rs2_recv,
    ret_send, ret_recv, own_grad, relay, relay2,
    part32, part, ax, as1, az, ay, agz, agx, bz, bs1, bx, by, bgx, bgz,
    load_sem, halo_sem, head_sem, rs_sem, ret_sem, hop_sem, hop2_sem,
    sax, saz, say, taz, tax, sbz, sbx, sby, tbx, tbz,
):
    pos = lax.axis_index("ctx")
    hi = lax.axis_index("head")
    x = pos % NX
    z = (pos // NX) % NZ
    y = pos // (NX * NZ)
    core = hi % 2
    far = hi // 2

    def at(ctx, head):
        return {"ctx": ctx, "head": head}

    right = at((pos + 1) % NCTX, hi)
    left = at((pos + NCTX - 1) % NCTX, hi)
    mate = far * 2 + (1 - core)
    twin = (1 - far) * 2 + core
    to_mate = at(pos, mate)

    def y_hop(d):
        p = (far * NY + y + d) % (2 * NY)
        head = (p // NY) * 2 + core
        return head, at(((p % NY) * NZ + z) * NX + x, head)

    (up_head, up), (down_head, down) = y_hop(2), y_hop(6)

    def x_peer(d):
        p = (x + d) % NX
        return p, at((y * NZ + z) * NX + p, hi)

    def z_peer(d):
        p = (z + d) % NZ
        return p, at((y * NZ + p) * NX + x, hi)

    def y_peer(d):
        p = (y + d) % NY
        return p, at((p * NZ + z) * NX + x, hi)

    started = []

    def send(src, dst_, sems, k, device):
        c = pltpu.make_async_remote_copy(
            src_ref=src, dst_ref=dst_, send_sem=sems.at[0, k], recv_sem=sems.at[1, k],
            device_id=device, device_id_type=MESH,
        )
        c.start()
        started.append(c)
        return c

    k_ref, v_ref = kw.at[ROWS : 2 * ROWS], vw.at[ROWS : 2 * ROWS]
    g_ref = gfull.at[:, span(hi, 256)]
    barrier = pltpu.get_barrier_semaphore()
    peers = [right, left, to_mate, up, down]
    peers += [x_peer(d)[1] for d in range(1, NX)]
    peers += [z_peer(d)[1] for d in range(1, NZ)]
    peers += [y_peer(d)[1] for d in range(1, NY)]
    for device in peers:
        pl.semaphore_signal(barrier, inc=1, device_id=device, device_id_type=MESH)
    pairs = ((k_hbm, k_ref), (v_hbm, v_ref), (g_hbm, g_ref), (q_hbm, q_ref), (w_hbm, w_ref))
    loads = [
        pltpu.make_async_copy(a, b, load_sem.at[i]) for i, (a, b) in enumerate(pairs)
    ]
    for c in loads:
        c.start()
    for c in loads:
        c.wait()
    pl.semaphore_wait(barrier, len(peers))

    halo = [
        send(k_ref, kw.at[0:ROWS], halo_sem, 0, right),
        send(k_ref, kw.at[2 * ROWS : 3 * ROWS], halo_sem, 1, left),
    ]
    quarter = lambda c: slice(c * BLK, (c + 1) * BLK)
    hops = [None] * 4
    for c in (0, 2, 1, 3):
        device = up if c < 2 else down
        hops[c] = send(g_ref.at[quarter(c)], relay.at[c], hop_sem, c, device)
    halo += [
        send(v_ref, vw.at[0:ROWS], halo_sem, 2, right),
        send(v_ref, vw.at[2 * ROWS : 3 * ROWS], halo_sem, 3, left),
    ]
    g_mate = send(g_ref, gfull.at[:, span(hi, 256)], head_sem, 1, to_mate)

    g_far = []
    rs2 = []

    def pass_on(c):
        hops[c].wait_recv()
        device, head = (up, down_head) if c < 2 else (down, up_head)
        g_far.append(
            send(relay.at[c], gfull.at[quarter(c), span(head, 256)], hop_sem, 4 + c, device)
        )

    tile = lists_ref[:, span(pos // 32, 128)].astype(F32)
    slot = lax.broadcasted_iota(jnp.int32, (8, BLK), 0)
    lane = lax.broadcasted_iota(jnp.int32, (8, BLK), 1)
    for n in range(4):
        row = jnp.max(
            jnp.where(lane == (pos % 32) * 4 + n, tile, -1.0), axis=1, keepdims=True
        )
        row = jnp.where(slot < counts_ref[pos * 4 + n], jnp.broadcast_to(row, (8, BLK)), -1.0)
        for wb in range(12):
            block = ((pos + NCTX - 1) * 4 + wb) % (NCTX * 4)
            hit = jnp.where(row == block.astype(F32), 1.0, 0.0)
            hit = jnp.max(hit, axis=0, keepdims=True)
            bias[wb : wb + 1, n * BLK : (n + 1) * BLK] = jnp.where(hit > 0.5, 0.0, -jnp.inf)

    factor = HD ** (-0.5)

    def score_chunk(h, c):
        hc = slice(h * HD, (h + 1) * HD)
        s = dot(kw[c * CHUNK : (c + 1) * CHUNK, hc], q_ref[:, hc], 1, 1) * (factor * LOG2E)
        for b in range(CHUNK // BLK):
            wb = c * (CHUNK // BLK) + b
            st[h, wb * BLK : (wb + 1) * BLK] = s[b * BLK : (b + 1) * BLK] + bias[wb : wb + 1]

    for h in range(HEADS_HERE):
        for c in (2, 3):
            score_chunk(h, c)
    pass_on(0)
    pass_on(2)
    halo[0].wait_recv()
    for h in range(HEADS_HERE):
        for c in (0, 1):
            score_chunk(h, c)
    pass_on(1)
    pass_on(3)
    halo[1].wait_recv()
    for h in range(HEADS_HERE):
        for c in (4, 5):
            score_chunk(h, c)
    for h in range(HEADS_HERE):
        top = jnp.max(st[h], axis=0, keepdims=True)
        total = jnp.zeros((1, ROWS), F32)
        for c in range(WINDOW // CHUNK):
            keys = slice(c * CHUNK, (c + 1) * CHUNK)
            e = jnp.exp2(st[h, keys] - top)
            st[h, keys] = e
            total = total + jnp.sum(e, axis=0, keepdims=True)
        inverse = 1.0 / total
        for c in range(WINDOW // CHUNK):
            keys = slice(c * CHUNK, (c + 1) * CHUNK)
            pt[h, keys] = (st[h, keys] * inverse).astype(BF)
    halo[2].wait_recv()
    halo[3].wait_recv()
    attn_t = []
    for h in range(HEADS_HERE):
        hc = slice(h * HD, (h + 1) * HD)
        mixed = dot(vw[:, hc], pt[h], 0, 0)
        attn_t.append(mixed.astype(BF))
        attn[:, hc] = jnp.transpose(mixed).astype(BF)

    g_share = []
    for c, got in zip((0, 2, 1, 3), g_far):
        got.wait_recv()
        view = gfull.at[quarter(c), span(twin, 256)]
        g_share.append(send(view, view, head_sem, 2 + c, to_mate))
    for f in range(2):
        cols = span(f * 2 + (1 - core), 256)
        rs_send[f] = dot(attn[...], w_ref[:, cols], 1, 0).astype(BF)
    rs = [send(rs_send.at[f], rs_recv.at[f], rs_sem, f, to_mate) for f in range(2)]
    for f in range(2):
        cols = span(f * 2 + core, 256)
        rs_keep[f] = dot(attn[...], w_ref[:, cols], 1, 0)
    g_mate.wait_recv()
    for c in g_share:
        c.wait_recv()

    for h in range(HEADS_HERE):
        value = dot(attn_t[h], gfull[...], 1, 0)
        part32[h * HD : (h + 1) * HD] = value
        part[h * HD : (h + 1) * HD] = value.astype(BF)
    cut = 4 * HD
    a_x, b_z = [], []
    for d in range(1, NX):
        p, device = x_peer(d)
        a_x.append(send(part.at[:, span(p, 128)], ax.at[d - 1], sax, d - 1, device))
    for d in range(1, NZ):
        p, device = z_peer(d)
        b_z.append(send(part.at[span(p, 32), cut:], bz.at[d - 1], sbz, d - 1, device))

    row_dots = []
    for h in range(HEADS_HERE):
        hc = slice(h * HD, (h + 1) * HD)
        back = dot(w_ref[hc], gfull[...], 1, 1).astype(BF).astype(F32)
        row_dots.append(jnp.sum(back * attn_t[h].astype(F32), axis=0, keepdims=True))
        ga[:, hc] = jnp.transpose(back).astype(BF)

    for c in rs:
        c.wait_recv()
    rs2_send[...] = (rs_keep[1 - far] + rs_recv[1 - far].astype(F32)).astype(BF)
    hops2 = [None] * 4
    for c in (0, 2, 1, 3):
        device = up if c < 2 else down
        hops2[c] = send(rs2_send.at[quarter(c)], relay2.at[c], hop2_sem, c, device)

    def pass_on2(c):
        hops2[c].wait_recv()
        rs2.append(
            send(relay2.at[c], rs2_recv.at[quarter(c)], hop2_sem, 4 + c, up if c < 2 else down)
        )

    def back_chunk(h, c):
        hc = slice(h * HD, (h + 1) * HD)
        keys = slice(c * CHUNK, (c + 1) * CHUNK)
        dp = dot(vw[keys, hc], ga[:, hc], 1, 1)
        ds = pt[h, keys].astype(F32) * ((dp - row_dots[h]) * factor)
        dst[h, keys] = ds.astype(BF)

    def key_grads(h, side):
        hc = slice(h * HD, (h + 1) * HD)
        keys = slice(side * ROWS, (side + 1) * ROWS)
        return dot(dst[h, keys], q_ref[:, hc], 1, 0), dot(pt[h, keys], ga[:, hc], 1, 0)

    rets = []
    for i, side, device in ((0, 2, right), (1, 0, left)):
        for h in range(HEADS_HERE):
            hc = slice(h * HD, (h + 1) * HD)
            for c in (side * 2, side * 2 + 1):
                back_chunk(h, c)
            dk, dv = key_grads(h, side)
            ret_send[i, 0, :, hc] = dk.astype(BF)
            ret_send[i, 1, :, hc] = dv.astype(BF)
        rets.append(send(ret_send.at[i, 0], ret_recv.at[i, 0], ret_sem, i, device))
        rets.append(send(ret_send.at[i, 1], ret_recv.at[i, 1], ret_sem, 2 + i, device))

    def total_of(first, copies, slots):
        value = first.astype(F32)
        for i, c in enumerate(copies):
            c.wait_recv()
            value = value + slots[i].astype(F32)
        return value.astype(BF)

    as1[...] = total_of(part32[:, span(x, 128)], a_x, ax)
    a_z = []
    for d in range(1, NZ):
        p, device = z_peer(d)
        a_z.append(send(as1.at[span(p, 32)], az.at[d - 1], saz, d - 1, device))
    bs1[...] = total_of(part32[span(z, 32), cut:], b_z, bz)
    b_x = []
    for d in range(1, NX):
        p, device = x_peer(d)
        b_x.append(send(bs1.at[:, span(p, 128)], bx.at[d - 1], sbx, d - 1, device))
    pass_on2(0)
    pass_on2(2)

    for h in range(HEADS_HERE):
        hc = slice(h * HD, (h + 1) * HD)
        for c in (2, 3):
            back_chunk(h, c)
        dk, dv = key_grads(h, 1)
        own_grad[0, :, hc] = dk
        own_grad[1, :, hc] = dv

    ay[y] = total_of(as1[span(z, 32)], a_z, az)
    a_y = [send(ay.at[y], ay.at[y], say, d - 1, y_peer(d)[1]) for d in range(1, NY)]
    by[y] = total_of(bs1[:, span(x, 128)], b_x, bx)
    b_y = [send(by.at[y], by.at[y], sby, d - 1, y_peer(d)[1]) for d in range(1, NY)]
    pass_on2(1)
    pass_on2(3)

    for h in range(HEADS_HERE):
        hc = slice(h * HD, (h + 1) * HD)
        grad = dot(kw[:, hc], dst[h], 0, 0)
        dq_ref[:, hc] = jnp.transpose(grad).astype(BF)

    def y_total(copies, slots):
        for c in copies:
            c.wait_recv()
        value = slots[0].astype(F32)
        for i in range(1, NY):
            value = value + slots[i].astype(F32)
        return value.astype(BF)

    agz[span(z, 32)] = y_total(a_y, ay)
    view = agz.at[span(z, 32)]
    a_gz = [send(view, view, taz, d - 1, z_peer(d)[1]) for d in range(1, NZ)]
    a_gx, b_gz = [], []

    def a_on(e):
        rows = span((z + NZ - e) % NZ, 32)
        for d in range(1, NX):
            to = agx.at[rows, span(x, 128)]
            a_gx.append(send(agz.at[rows], to, tax, e * (NX - 1) + d - 1, x_peer(d)[1]))

    def b_on(e):
        cols = span((x + NX - e) % NX, 128)
        for d in (4, 3, 5, 2, 6, 1, 7):
            to = bgz.at[span(z, 32), cols]
            b_gz.append(send(bgx.at[:, cols], to, tbz, e * (NZ - 1) + d - 1, z_peer(d)[1]))

    bgx[:, span(x, 128)] = y_total(b_y, by)
    view_b = bgx.at[:, span(x, 128)]
    b_gx = [send(view_b, view_b, tbx, d - 1, x_peer(d)[1]) for d in range(1, NX)]
    b_on(0)
    a_on(0)
    for e in (1, 3, 2):
        b_gx[e - 1].wait_recv()
        b_on(e)
    bgz[span(z, 32)] = bgx[...]
    for e in (1, 7, 2, 6, 3, 5, 4):
        a_gz[e - 1].wait_recv()
        a_on(e)
    agx[:, span(x, 128)] = agz[...]

    for c in rs2:
        c.wait_recv()
    out_ref[...] = (
        rs_keep[far] + rs_recv[far].astype(F32) + rs2_recv[...].astype(F32)
    ).astype(BF)
    for c in rets:
        c.wait_recv()
    for i, ref in ((0, dk_ref), (1, dv_ref)):
        ref[...] = (
            own_grad[i] + ret_recv[0, i].astype(F32) + ret_recv[1, i].astype(F32)
        ).astype(BF)
    scale = (NCTX * ROWS) ** (-0.5)
    for c in b_gz:
        c.wait_recv()
    dw_ref[:, cut:] = bgz[...].astype(F32) * scale
    for c in a_gx:
        c.wait_recv()
    dw_ref[:, :cut] = agx[...].astype(F32) * scale
    for c in started:
        c.wait_send()


def hand_out_kernel(*refs):
    n = len(refs) // 3
    sources, targets, held = refs[:n], refs[n : 2 * n], refs[2 * n : 3 * n]
    sem = refs[3 * n]
    reads = [pltpu.make_async_copy(sources[i], held[i], sem.at[0, i]) for i in range(n)]
    writes = [pltpu.make_async_copy(held[i], targets[i], sem.at[1, i]) for i in range(n)]
    for c in reads:
        c.start()
    for i in range(n):
        reads[i].wait()
        writes[i].start()
    for c in writes:
        c.wait()


def hand_out(arrays):
    shapes = [jax.ShapeDtypeStruct(a.shape, a.dtype) for a in arrays]
    n = len(arrays)
    hbm = pl.BlockSpec(memory_space=pl.ANY)
    return pl.pallas_call(
        hand_out_kernel,
        out_shape=shapes,
        in_specs=[hbm] * n,
        out_specs=[hbm] * n,
        scratch_shapes=[pltpu.VMEM(a.shape, a.dtype) for a in arrays]
        + [pltpu.SemaphoreType.DMA((2, n))],
        name="hand_out",
    )(*arrays)


def shards(queries, keys, values, out_weight, grad_output, key_lists, key_counts):
    vmem = pl.BlockSpec(memory_space=pltpu.VMEM)
    smem = pl.BlockSpec(memory_space=pltpu.SMEM)
    dma = lambda n: pltpu.SemaphoreType.DMA((2, n))
    tok = jax.ShapeDtypeStruct(queries.shape, BF)
    results = pl.pallas_call(
        layer_kernel,
        out_shape=(tok, tok, tok, tok, jax.ShapeDtypeStruct(out_weight.shape, F32)),
        in_specs=[pl.BlockSpec(memory_space=pl.ANY)] * 5 + [vmem, smem],
        out_specs=[vmem] * 5,
        scratch_shapes=[
            pltpu.VMEM((ROWS, 256), BF),
            pltpu.VMEM((256, 1024), BF),
            pltpu.VMEM((WINDOW, 256), BF),
            pltpu.VMEM((WINDOW, 256), BF),
            pltpu.VMEM((16, ROWS), F32),
            pltpu.VMEM((HEADS_HERE, WINDOW, ROWS), F32),
            pltpu.VMEM((HEADS_HERE, WINDOW, ROWS), BF),
            pltpu.VMEM((HEADS_HERE, WINDOW, ROWS), BF),
            pltpu.VMEM((ROWS, 256), BF),
            pltpu.VMEM((ROWS, 256), BF),
            pltpu.VMEM((ROWS, 1024), BF),
            pltpu.VMEM((2, ROWS, 256), BF),
            pltpu.VMEM((2, ROWS, 256), BF),
            pltpu.VMEM((2, ROWS, 256), F32),
            pltpu.VMEM((ROWS, 256), BF),
            pltpu.VMEM((ROWS, 256), BF),
            pltpu.VMEM((2, 2, ROWS, 256), BF),
            pltpu.VMEM((2, 2, ROWS, 256), BF),
            pltpu.VMEM((2, ROWS, 256), F32),
            pltpu.VMEM((4, BLK, 256), BF),
            pltpu.VMEM((4, BLK, 256), BF),
            pltpu.VMEM((256, 1024), F32),
            pltpu.VMEM((256, 1024), BF),
            pltpu.VMEM((NX - 1, 256, 128), BF),
            pltpu.VMEM((256, 128), BF),
            pltpu.VMEM((NZ - 1, 32, 128), BF),
            pltpu.VMEM((NY, 32, 128), BF),
            pltpu.VMEM((256, 128), BF),
            pltpu.VMEM((256, 512), BF),
            pltpu.VMEM((NZ - 1, 32, 512), BF),
            pltpu.VMEM((32, 512), BF),
            pltpu.VMEM((NX - 1, 32, 128), BF),
            pltpu.VMEM((NY, 32, 128), BF),
            pltpu.VMEM((32, 512), BF),
            pltpu.VMEM((256, 512), BF),
            pltpu.SemaphoreType.DMA((5,)), dma(4), dma(6), dma(2), dma(4), dma(8), dma(8),
            dma(NX - 1), dma(NZ - 1), dma(NY - 1), dma(NZ - 1), dma(NZ * (NX - 1)),
            dma(NZ - 1), dma(NX - 1), dma(NY - 1), dma(NX - 1), dma(NX * (NZ - 1)),
        ],
        compiler_params=pltpu.CompilerParams(
            collective_id=0, has_side_effects=True, vmem_limit_bytes=62 * 1024 * 1024
        ),
        name="layer",
    )(queries, keys, values, out_weight, grad_output, key_lists.T, key_counts)
    return hand_out(results)


def solution(mesh):
    in_specs = (
        P("ctx", "head"),
        P("ctx", "head"),
        P("ctx", "head"),
        P("head", None),
        P("ctx", "head"),
        P(),
        P(),
    )
    out_specs = (
        P("ctx", "head"),
        P("ctx", "head"),
        P("ctx", "head"),
        P("ctx", "head"),
        P("head", None),
    )
    return jax.shard_map(shards, mesh=mesh, in_specs=in_specs, out_specs=out_specs, check_vma=False)
```

```python
import jax
import jax.numpy as jnp
from jax import lax
from jax.experimental import pallas as pl
from jax.experimental.pallas import tpu as pltpu
from jax.sharding import PartitionSpec as P

HD = 128
BLK = 128
MESH = pl.DeviceIdType.MESH
BF = jnp.bfloat16
F32 = jnp.float32
NY, NZ, NX = 4, 8, 4
NCTX = NY * NZ * NX
LOG2E = 1.4426950408889634
HEADS_HERE = 2
ROWS = 512
WINDOW = 3 * ROWS
CHUNK = 256


def dot(a, b, ca, cb):
    return lax.dot_general(a, b, (((ca,), (cb,)), ((), ())), preferred_element_type=F32)


def span(i, n):
    return pl.ds(pl.multiple_of(i * n, n), n)


def layer_kernel(
    q_hbm, k_hbm, v_hbm, w_hbm, g_hbm, lists_ref, counts_ref,
    out_ref, dq_ref, dk_ref, dv_ref, dw_ref,
    q_ref, w_ref,
    kw, vw, bias, st, pt, dst, attn, ga, gfull,
    rs_send, rs_recv, rs_keep, rs2_send, rs2_recv,
    ret_send, ret_recv, own_grad, relay, relay2,
    part32, part, ax, as1, az, ay, agz, agx, bz, bs1, bx, by, bgx, bgz,
    load_sem, halo_sem, head_sem, rs_sem, ret_sem, hop_sem, hop2_sem,
    sax, saz, say, taz, tax, sbz, sbx, sby, tbx, tbz,
):
    pos = lax.axis_index("ctx")
    hi = lax.axis_index("head")
    x = pos % NX
    z = (pos // NX) % NZ
    y = pos // (NX * NZ)
    core = hi % 2
    far = hi // 2

    def at(ctx, head):
        return {"ctx": ctx, "head": head}

    right = at((pos + 1) % NCTX, hi)
    left = at((pos + NCTX - 1) % NCTX, hi)
    mate = far * 2 + (1 - core)
    twin = (1 - far) * 2 + core
    to_mate = at(pos, mate)

    def y_hop(d):
        p = (far * NY + y + d) % (2 * NY)
        head = (p // NY) * 2 + core
        return head, at(((p % NY) * NZ + z) * NX + x, head)

    (up_head, up), (down_head, down) = y_hop(2), y_hop(6)

    def x_peer(d):
        p = (x + d) % NX
        return p, at((y * NZ + z) * NX + p, hi)

    def z_peer(d):
        p = (z + d) % NZ
        return p, at((y * NZ + p) * NX + x, hi)

    def y_peer(d):
        p = (y + d) % NY
        return p, at((p * NZ + z) * NX + x, hi)

    started = []

    def send(src, dst_, sems, k, device):
        c = pltpu.make_async_remote_copy(
            src_ref=src, dst_ref=dst_, send_sem=sems.at[0, k], recv_sem=sems.at[1, k],
            device_id=device, device_id_type=MESH,
        )
        c.start()
        started.append(c)
        return c

    k_ref, v_ref = kw.at[ROWS : 2 * ROWS], vw.at[ROWS : 2 * ROWS]
    g_ref = gfull.at[:, span(hi, 256)]
    barrier = pltpu.get_barrier_semaphore()
    peers = [right, left, to_mate, up, down]
    peers += [x_peer(d)[1] for d in range(1, NX)]
    peers += [z_peer(d)[1] for d in range(1, NZ)]
    peers += [y_peer(d)[1] for d in range(1, NY)]
    for device in peers:
        pl.semaphore_signal(barrier, inc=1, device_id=device, device_id_type=MESH)
    pairs = ((k_hbm, k_ref), (v_hbm, v_ref), (g_hbm, g_ref), (q_hbm, q_ref), (w_hbm, w_ref))
    loads = [
        pltpu.make_async_copy(a, b, load_sem.at[i]) for i, (a, b) in enumerate(pairs)
    ]
    for c in loads:
        c.start()
    for c in loads:
        c.wait()
    pl.semaphore_wait(barrier, len(peers))

    halo = [
        send(k_ref, kw.at[0:ROWS], halo_sem, 0, right),
        send(k_ref, kw.at[2 * ROWS : 3 * ROWS], halo_sem, 1, left),
    ]
    quarter = lambda c: slice(c * BLK, (c + 1) * BLK)
    hops = [None] * 4
    halo += [
        send(v_ref, vw.at[0:ROWS], halo_sem, 2, right),
        send(v_ref, vw.at[2 * ROWS : 3 * ROWS], halo_sem, 3, left),
    ]
    g_mate = send(g_ref, gfull.at[:, span(hi, 256)], head_sem, 1, to_mate)

    g_far = []
    rs2 = []

    def pass_on(c):
        hops[c].wait_recv()
        device, head = (up, down_head) if c < 2 else (down, up_head)
        g_far.append(
            send(relay.at[c], gfull.at[quarter(c), span(head, 256)], hop_sem, 4 + c, device)
        )

    tile = lists_ref[:, span(pos // 32, 128)].astype(F32)
    slot = lax.broadcasted_iota(jnp.int32, (8, BLK), 0)
    lane = lax.broadcasted_iota(jnp.int32, (8, BLK), 1)
    for n in range(4):
        row = jnp.max(
            jnp.where(lane == (pos % 32) * 4 + n, tile, -1.0), axis=1, keepdims=True
        )
        row = jnp.where(slot < counts_ref[pos * 4 + n], jnp.broadcast_to(row, (8, BLK)), -1.0)
        for wb in range(12):
            block = ((pos + NCTX - 1) * 4 + wb) % (NCTX * 4)
            hit = jnp.where(row == block.astype(F32), 1.0, 0.0)
            hit = jnp.max(hit, axis=0, keepdims=True)
            bias[wb : wb + 1, n * BLK : (n + 1) * BLK] = jnp.where(hit > 0.5, 0.0, -jnp.inf)

    factor = HD ** (-0.5)

    def score_chunk(h, c):
        hc = slice(h * HD, (h + 1) * HD)
        s = dot(kw[c * CHUNK : (c + 1) * CHUNK, hc], q_ref[:, hc], 1, 1) * (factor * LOG2E)
        for b in range(CHUNK // BLK):
            wb = c * (CHUNK // BLK) + b
            st[h, wb * BLK : (wb + 1) * BLK] = s[b * BLK : (b + 1) * BLK] + bias[wb : wb + 1]

    for h in range(HEADS_HERE):
        for c in (2, 3):
            score_chunk(h, c)
    halo[0].wait_recv()
    for c in (0, 2, 1, 3):
        device = up if c < 2 else down
        hops[c] = send(g_ref.at[quarter(c)], relay.at[c], hop_sem, c, device)
    for h in range(HEADS_HERE):
        for c in (0, 1):
            score_chunk(h, c)
    halo[1].wait_recv()
    for h in range(HEADS_HERE):
        for c in (4, 5):
            score_chunk(h, c)
    for h in range(HEADS_HERE):
        top = jnp.max(st[h], axis=0, keepdims=True)
        total = jnp.zeros((1, ROWS), F32)
        for c in range(WINDOW // CHUNK):
            keys = slice(c * CHUNK, (c + 1) * CHUNK)
            e = jnp.exp2(st[h, keys] - top)
            st[h, keys] = e
            total = total + jnp.sum(e, axis=0, keepdims=True)
        inverse = 1.0 / total
        for c in range(WINDOW // CHUNK):
            keys = slice(c * CHUNK, (c + 1) * CHUNK)
            pt[h, keys] = (st[h, keys] * inverse).astype(BF)
    pass_on(0)
    pass_on(2)
    halo[2].wait_recv()
    halo[3].wait_recv()
    pass_on(1)
    pass_on(3)
    attn_t = []
    for h in range(HEADS_HERE):
        hc = slice(h * HD, (h + 1) * HD)
        mixed = dot(vw[:, hc], pt[h], 0, 0)
        attn_t.append(mixed.astype(BF))
        attn[:, hc] = jnp.transpose(mixed).astype(BF)

    g_share = []
    for c, got in zip((0, 2, 1, 3), g_far):
        got.wait_recv()
        view = gfull.at[quarter(c), span(twin, 256)]
        g_share.append(send(view, view, head_sem, 2 + c, to_mate))
    for f in range(2):
        cols = span(f * 2 + (1 - core), 256)
        rs_send[f] = dot(attn[...], w_ref[:, cols], 1, 0).astype(BF)
    rs = [send(rs_send.at[f], rs_recv.at[f], rs_sem, f, to_mate) for f in range(2)]
    for f in range(2):
        cols = span(f * 2 + core, 256)
        rs_keep[f] = dot(attn[...], w_ref[:, cols], 1, 0)
    g_mate.wait_recv()
    for c in g_share:
        c.wait_recv()

    for h in range(HEADS_HERE):
        value = dot(attn_t[h], gfull[...], 1, 0)
        part32[h * HD : (h + 1) * HD] = value
        part[h * HD : (h + 1) * HD] = value.astype(BF)
    cut = 4 * HD
    a_x, b_z = [], []
    for d in range(1, NX):
        p, device = x_peer(d)
        a_x.append(send(part.at[:, span(p, 128)], ax.at[d - 1], sax, d - 1, device))
    for d in range(1, NZ):
        p, device = z_peer(d)
        b_z.append(send(part.at[span(p, 32), cut:], bz.at[d - 1], sbz, d - 1, device))

    row_dots = []
    for h in range(HEADS_HERE):
        hc = slice(h * HD, (h + 1) * HD)
        back = dot(w_ref[hc], gfull[...], 1, 1).astype(BF).astype(F32)
        row_dots.append(jnp.sum(back * attn_t[h].astype(F32), axis=0, keepdims=True))
        ga[:, hc] = jnp.transpose(back).astype(BF)

    for c in rs:
        c.wait_recv()
    rs2_send[...] = (rs_keep[1 - far] + rs_recv[1 - far].astype(F32)).astype(BF)
    hops2 = [None] * 4
    for c in (0, 2, 1, 3):
        device = up if c < 2 else down
        hops2[c] = send(rs2_send.at[quarter(c)], relay2.at[c], hop2_sem, c, device)

    def pass_on2(c):
        hops2[c].wait_recv()
        rs2.append(
            send(relay2.at[c], rs2_recv.at[quarter(c)], hop2_sem, 4 + c, up if c < 2 else down)
        )

    def back_chunk(h, c):
        hc = slice(h * HD, (h + 1) * HD)
        keys = slice(c * CHUNK, (c + 1) * CHUNK)
        dp = dot(vw[keys, hc], ga[:, hc], 1, 1)
        ds = pt[h, keys].astype(F32) * ((dp - row_dots[h]) * factor)
        dst[h, keys] = ds.astype(BF)

    def key_grads(h, side):
        hc = slice(h * HD, (h + 1) * HD)
        keys = slice(side * ROWS, (side + 1) * ROWS)
        return dot(dst[h, keys], q_ref[:, hc], 1, 0), dot(pt[h, keys], ga[:, hc], 1, 0)

    rets = []
    for i, side, device in ((0, 2, right), (1, 0, left)):
        for h in range(HEADS_HERE):
            hc = slice(h * HD, (h + 1) * HD)
            for c in (side * 2, side * 2 + 1):
                back_chunk(h, c)
            dk, dv = key_grads(h, side)
            ret_send[i, 0, :, hc] = dk.astype(BF)
            ret_send[i, 1, :, hc] = dv.astype(BF)
        rets.append(send(ret_send.at[i, 0], ret_recv.at[i, 0], ret_sem, i, device))
        rets.append(send(ret_send.at[i, 1], ret_recv.at[i, 1], ret_sem, 2 + i, device))

    def total_of(first, copies, slots):
        value = first.astype(F32)
        for i, c in enumerate(copies):
            c.wait_recv()
            value = value + slots[i].astype(F32)
        return value.astype(BF)

    as1[...] = total_of(part32[:, span(x, 128)], a_x, ax)
    a_z = []
    for d in range(1, NZ):
        p, device = z_peer(d)
        a_z.append(send(as1.at[span(p, 32)], az.at[d - 1], saz, d - 1, device))
    bs1[...] = total_of(part32[span(z, 32), cut:], b_z, bz)
    b_x = []
    for d in range(1, NX):
        p, device = x_peer(d)
        b_x.append(send(bs1.at[:, span(p, 128)], bx.at[d - 1], sbx, d - 1, device))
    pass_on2(0)
    pass_on2(2)

    for h in range(HEADS_HERE):
        hc = slice(h * HD, (h + 1) * HD)
        for c in (2, 3):
            back_chunk(h, c)
        dk, dv = key_grads(h, 1)
        own_grad[0, :, hc] = dk
        own_grad[1, :, hc] = dv

    ay[y] = total_of(as1[span(z, 32)], a_z, az)
    a_y = [send(ay.at[y], ay.at[y], say, d - 1, y_peer(d)[1]) for d in range(1, NY)]
    by[y] = total_of(bs1[:, span(x, 128)], b_x, bx)
    b_y = [send(by.at[y], by.at[y], sby, d - 1, y_peer(d)[1]) for d in range(1, NY)]
    pass_on2(1)
    pass_on2(3)

    for h in range(HEADS_HERE):
        hc = slice(h * HD, (h + 1) * HD)
        grad = dot(kw[:, hc], dst[h], 0, 0)
        dq_ref[:, hc] = jnp.transpose(grad).astype(BF)

    def y_total(copies, slots):
        for c in copies:
            c.wait_recv()
        value = slots[0].astype(F32)
        for i in range(1, NY):
            value = value + slots[i].astype(F32)
        return value.astype(BF)

    agz[span(z, 32)] = y_total(a_y, ay)
    view = agz.at[span(z, 32)]
    a_gz = [send(view, view, taz, d - 1, z_peer(d)[1]) for d in range(1, NZ)]
    bgx[:, span(x, 128)] = y_total(b_y, by)
    view_b = bgx.at[:, span(x, 128)]
    b_gx = [send(view_b, view_b, tbx, d - 1, x_peer(d)[1]) for d in range(1, NX)]
    for c in b_gx:
        c.wait_recv()
    b_gz = [send(bgx, bgz.at[span(z, 32)], tbz, d - 1, z_peer(d)[1]) for d in range(1, NZ)]
    bgz[span(z, 32)] = bgx[...]
    for c in a_gz:
        c.wait_recv()
    a_gx = [send(agz, agx.at[:, span(x, 128)], tax, d - 1, x_peer(d)[1]) for d in range(1, NX)]
    agx[:, span(x, 128)] = agz[...]

    for c in rs2:
        c.wait_recv()
    out_ref[...] = (
        rs_keep[far] + rs_recv[far].astype(F32) + rs2_recv[...].astype(F32)
    ).astype(BF)
    for c in rets:
        c.wait_recv()
    for i, ref in ((0, dk_ref), (1, dv_ref)):
        ref[...] = (
            own_grad[i] + ret_recv[0, i].astype(F32) + ret_recv[1, i].astype(F32)
        ).astype(BF)
    scale = (NCTX * ROWS) ** (-0.5)
    for c in b_gz:
        c.wait_recv()
    dw_ref[:, cut:] = bgz[...].astype(F32) * scale
    for c in a_gx:
        c.wait_recv()
    dw_ref[:, :cut] = agx[...].astype(F32) * scale
    for c in started:
        c.wait_send()


def hand_out_kernel(*refs):
    n = len(refs) // 3
    sources, targets, held = refs[:n], refs[n : 2 * n], refs[2 * n : 3 * n]
    sem = refs[3 * n]
    reads = [pltpu.make_async_copy(sources[i], held[i], sem.at[0, i]) for i in range(n)]
    writes = [pltpu.make_async_copy(held[i], targets[i], sem.at[1, i]) for i in range(n)]
    for c in reads:
        c.start()
    for i in range(n):
        reads[i].wait()
        writes[i].start()
    for c in writes:
        c.wait()


def hand_out(arrays):
    shapes = [jax.ShapeDtypeStruct(a.shape, a.dtype) for a in arrays]
    n = len(arrays)
    hbm = pl.BlockSpec(memory_space=pl.ANY)
    return pl.pallas_call(
        hand_out_kernel,
        out_shape=shapes,
        in_specs=[hbm] * n,
        out_specs=[hbm] * n,
        scratch_shapes=[pltpu.VMEM(a.shape, a.dtype) for a in arrays]
        + [pltpu.SemaphoreType.DMA((2, n))],
        name="hand_out",
    )(*arrays)


def shards(queries, keys, values, out_weight, grad_output, key_lists, key_counts):
    vmem = pl.BlockSpec(memory_space=pltpu.VMEM)
    smem = pl.BlockSpec(memory_space=pltpu.SMEM)
    dma = lambda n: pltpu.SemaphoreType.DMA((2, n))
    tok = jax.ShapeDtypeStruct(queries.shape, BF)
    results = pl.pallas_call(
        layer_kernel,
        out_shape=(tok, tok, tok, tok, jax.ShapeDtypeStruct(out_weight.shape, F32)),
        in_specs=[pl.BlockSpec(memory_space=pl.ANY)] * 5 + [vmem, smem],
        out_specs=[vmem] * 5,
        scratch_shapes=[
            pltpu.VMEM((ROWS, 256), BF),
            pltpu.VMEM((256, 1024), BF),
            pltpu.VMEM((WINDOW, 256), BF),
            pltpu.VMEM((WINDOW, 256), BF),
            pltpu.VMEM((16, ROWS), F32),
            pltpu.VMEM((HEADS_HERE, WINDOW, ROWS), F32),
            pltpu.VMEM((HEADS_HERE, WINDOW, ROWS), BF),
            pltpu.VMEM((HEADS_HERE, WINDOW, ROWS), BF),
            pltpu.VMEM((ROWS, 256), BF),
            pltpu.VMEM((ROWS, 256), BF),
            pltpu.VMEM((ROWS, 1024), BF),
            pltpu.VMEM((2, ROWS, 256), BF),
            pltpu.VMEM((2, ROWS, 256), BF),
            pltpu.VMEM((2, ROWS, 256), F32),
            pltpu.VMEM((ROWS, 256), BF),
            pltpu.VMEM((ROWS, 256), BF),
            pltpu.VMEM((2, 2, ROWS, 256), BF),
            pltpu.VMEM((2, 2, ROWS, 256), BF),
            pltpu.VMEM((2, ROWS, 256), F32),
            pltpu.VMEM((4, BLK, 256), BF),
            pltpu.VMEM((4, BLK, 256), BF),
            pltpu.VMEM((256, 1024), F32),
            pltpu.VMEM((256, 1024), BF),
            pltpu.VMEM((NX - 1, 256, 128), BF),
            pltpu.VMEM((256, 128), BF),
            pltpu.VMEM((NZ - 1, 32, 128), BF),
            pltpu.VMEM((NY, 32, 128), BF),
            pltpu.VMEM((256, 128), BF),
            pltpu.VMEM((256, 512), BF),
            pltpu.VMEM((NZ - 1, 32, 512), BF),
            pltpu.VMEM((32, 512), BF),
            pltpu.VMEM((NX - 1, 32, 128), BF),
            pltpu.VMEM((NY, 32, 128), BF),
            pltpu.VMEM((32, 512), BF),
            pltpu.VMEM((256, 512), BF),
            pltpu.SemaphoreType.DMA((5,)), dma(4), dma(6), dma(2), dma(4), dma(8), dma(8),
            dma(NX - 1), dma(NZ - 1), dma(NY - 1), dma(NZ - 1), dma(NZ * (NX - 1)),
            dma(NZ - 1), dma(NX - 1), dma(NY - 1), dma(NX - 1), dma(NX * (NZ - 1)),
        ],
        compiler_params=pltpu.CompilerParams(
            collective_id=0, has_side_effects=True, vmem_limit_bytes=62 * 1024 * 1024
        ),
        name="layer",
    )(queries, keys, values, out_weight, grad_output, key_lists.T, key_counts)
    return hand_out(results)


def solution(mesh):
    in_specs = (
        P("ctx", "head"),
        P("ctx", "head"),
        P("ctx", "head"),
        P("head", None),
        P("ctx", "head"),
        P(),
        P(),
    )
    out_specs = (
        P("ctx", "head"),
        P("ctx", "head"),
        P("ctx", "head"),
        P("ctx", "head"),
        P("head", None),
    )
    return jax.shard_map(shards, mesh=mesh, in_specs=in_specs, out_specs=out_specs, check_vma=False)
```
